32 devices in a mesh: gx: 4 (over z), gy: 4 (over y, core), gz: 2 (over x).
Axes of the slice: x: 2, y: 2, z: 4, core: 2. Of those that a mesh axis runs over, the one named last changes fastest.
Arguments:
- velocities: float32 [3, 1310720], P(None, ('gx', 'gy', 'gz')), may hold values from -6 to 6
- particle_cells: int32 [2, 1310720], P(None, ('gx', 'gy', 'gz')), may hold values from 0 to 4095
- grid_shift: int32 [2, 3], replicated, may hold values from -1 to 1, as said below
- axis_index: int32 [2, 16, 32, 256], P(None, 'gx', 'gy', 'gz'), may hold values from 0 to 7
- migrate_dir: int32 [1310720], P(('gx', 'gy', 'gz')), may hold values from 0 to 6, as said below
- migrate_slot: int32 [1310720], P(('gx', 'gy', 'gz')), may hold values from 0 to 159, as said below
- contact_colloid: int32 [65536], P(('gx', 'gy', 'gz')), may hold values from 0 to 8191, as said below
- contact_particle: int32 [65536], P(('gx', 'gy', 'gz')), may hold values from 0 to 40959
- contact_weight: float32 [65536], P(('gx', 'gy', 'gz')), may hold values from 0.05 to 1
- colloid_velocity: float32 [3, 8192], P(None, ('gx', 'gy', 'gz')), may hold values from -6 to 6
Outputs:
- cell_velocity: float32 [3, 16, 32, 256], P(None, 'gx', 'gy', 'gz')
- migrated: float32 [3, 1341440], P(None, ('gx', 'gy', 'gz'))
- colloid_force: float32 [3, 8192], P(None, ('gx', 'gy', 'gz'))
The draws below stay inside these ranges and needn't reach their ends.
Inputs may be any that keep to these rules, and one draw needn't show every extreme that they name: `grid_shift`: every entry is -1 or 1, and along every dimension the sign changes from each step to the next. `migrate_dir`: code 0 keeps a particle on its device. On every device at most 160 particles take any one nonzero code, and on every device some nonzero code is taken by exactly 160 particles. `migrate_slot`: among the particles of one device with the same nonzero code, the slots are distinct and run from 0 to that code's count minus 1; the slot is 0 where the code is 0. `contact_colloid`: the owner of every contact's colloid is the contact's own device or one of its six face neighbours along gx, gy, gz (periodic).
All inputs are finite; a program needn't handle non-finite values.
Results may differ from the reference program's by a relative error of at most 0.00015.
Values sent between devices are 32-bit elements; how exact they have to be, the bound alone decides.
A program may use at most 128 MiB of HBM per device.

```python
import math
import jax
import jax.numpy as jnp
import numpy as np

CX = 4
CY = 8
CZ = 128
STEPS = 2
COLLOIDS_PER_UNIT = 256
P_DEV = 40960
CAP = 160
CONTACTS_PER_UNIT = 2048
NX = 16
NY = 32
NZ = 256
PARTICLES = 1310720
COLLOIDS = 8192
CONTACTS = 65536
N_GX = 4
N_GY = 4
N_GZ = 2


def draw_grid_shift(key, part):
    signs = 2 * jax.random.randint(jax.random.fold_in(key, 3), (3,), 0, 2) - 1
    flips = jnp.where(jnp.arange(STEPS) % 2 == 0, 1, -1)
    return (flips[:, None] * signs[None, :]).astype(jnp.int32)


def migration_codes(key):
    base = jax.random.fold_in(key, 7)
    device_list = PARTICLES // P_DEV

    def device_codes(device):
        device_key = jax.random.fold_in(base, device)
        key_count, key_forced, key_order = jax.random.split(device_key, 3)
        counts = jax.random.randint(key_count, (6,), CAP // 4, CAP + 1)
        forced = jax.random.randint(key_forced, (), 0, 6)
        counts = jnp.where(jnp.arange(6) == forced, CAP, counts)
        ends = jnp.cumsum(counts)
        starts = ends - counts
        rank = jnp.arange(P_DEV)
        inside = rank < ends[5]
        number = jnp.sum((rank[:, None] >= ends[None, :]).astype(jnp.int32), axis=1)
        codes = jnp.where(inside, 1 + number, 0).astype(jnp.int32)
        places = jnp.where(inside, rank - starts[jnp.clip(number, 0, 5)], 0).astype(jnp.int32)
        order = jax.random.permutation(key_order, P_DEV)
        dirs = jnp.zeros((P_DEV,), jnp.int32).at[order].set(codes)
        slots = jnp.zeros((P_DEV,), jnp.int32).at[order].set(places)
        return (dirs, slots)
    dirs, slots = jax.vmap(device_codes)(jnp.arange(device_list))
    return (dirs.reshape(-1), slots.reshape(-1))


def draw_migrate_dir(key, part):
    return migration_codes(key)[0]


def draw_migrate_slot(key, part):
    return migration_codes(key)[1]


def draw_contact_colloid(key, part):
    grid_x = NX // CX
    grid_y = NY // CY
    grid_z = NZ // CZ
    device_list = grid_x * grid_y * grid_z
    key_near, member_key = jax.random.split(jax.random.fold_in(key, 11))
    neighbour = jax.random.randint(key_near, (device_list, CONTACTS_PER_UNIT), 0, 7)
    member_index = jax.random.randint(member_key, (device_list, CONTACTS_PER_UNIT), 0, COLLOIDS_PER_UNIT)
    moves = jnp.asarray(np.array([[0, 0, 0], [1, 0, 0], [-1, 0, 0], [0, 1, 0], [0, -1, 0], [0, 0, 1], [0, 0, -1]], dtype=np.int32))
    offsets = moves[neighbour]
    device = jnp.arange(device_list, dtype=jnp.int32)[:, None]
    place_x = device // (grid_y * grid_z)
    place_y = device // grid_z % grid_y
    place_z = device % grid_z
    owning_device = ((place_x + offsets[..., 0]) % grid_x * grid_y + (place_y + offsets[..., 1]) % grid_y) * grid_z + (place_z + offsets[..., 2]) % grid_z
    return (owning_device * COLLOIDS_PER_UNIT + member_index).reshape(-1).astype(jnp.int32)


def place_ends(values, own_key, least, high):
    dims = values.shape
    place = [jax.random.randint(jax.random.fold_in(own_key, axis), (), 0, dims[axis]) for axis in range(len(dims))]
    values = values.at[tuple(place)].set(least)
    longest = dims.index(max(dims))
    place[longest] = (place[longest] + 1) % dims[longest]
    return values.at[tuple(place)].set(high)


def block_levels(stream_key, dims, pieces, least, top_value):
    gain = 1.0
    for axis_at, parts in pieces:
        draws = jax.random.uniform(jax.random.fold_in(jax.random.fold_in(stream_key, 6), axis_at), (parts,), jnp.float32, least / len(pieces), top_value / len(pieces))
        gain = gain * jnp.repeat(jnp.exp(draws), dims[axis_at] // parts).reshape((-1,) + (1,) * (len(dims) - 1 - axis_at))
    return gain


def noise(rng, shape, deviation, limit, shards=(), kind=jnp.bfloat16):
    result = deviation * jax.random.normal(rng, shape, jnp.float32)
    if shards:
        result = result * block_levels(rng, shape, shards, -0.22, 0.18)
    return jnp.clip(result, -limit, limit).astype(kind)


def setup_inputs(seed: int = 0) -> dict:
    keys = jax.random.split(jax.random.key(seed), 11)
    velocities = noise(keys[0], (3, PARTICLES), 1.0, 6.0, ((1, 32),), jnp.float32)
    particle_cells = place_ends(jax.random.randint(keys[1], (STEPS, PARTICLES), 0, CX * CY * CZ), jax.random.fold_in(keys[1], 1), 0, (CX * CY * CZ) - 1).astype(jnp.int32)
    grid_shift = draw_grid_shift(jax.random.fold_in(keys[10], 71), 0)
    axis_index = place_ends(jax.random.randint(keys[3], (STEPS, NX, NY, NZ), 0, 8), jax.random.fold_in(keys[3], 1), 0, 7).astype(jnp.int32)
    migrate_dir = draw_migrate_dir(jax.random.fold_in(keys[10], 71), 0)
    migrate_slot = draw_migrate_slot(jax.random.fold_in(keys[10], 71), 0)
    contact_colloid = draw_contact_colloid(jax.random.fold_in(keys[10], 71), 0)
    contact_particle = place_ends(jax.random.randint(keys[7], (CONTACTS,), 0, P_DEV), jax.random.fold_in(keys[7], 1), 0, P_DEV - 1).astype(jnp.int32)
    contact_weight = jnp.clip(jnp.exp(math.log(1.0) - 2.9957323 * jax.random.uniform(keys[8], (CONTACTS,), jnp.float32) ** block_levels(keys[8], (CONTACTS,), ((0, 32),), -0.2, 0.2)), 0.05, 1.0)
    colloid_velocity = noise(keys[9], (3, COLLOIDS), 1.0, 6.0, ((1, 32),), jnp.float32)
    return dict(velocities=velocities, particle_cells=particle_cells, grid_shift=grid_shift, axis_index=axis_index, migrate_dir=migrate_dir, migrate_slot=migrate_slot, contact_colloid=contact_colloid, contact_particle=contact_particle, contact_weight=contact_weight, colloid_velocity=colloid_velocity)


def rotation_table():
    angle = 130.0 * math.pi / 180.0
    cosine = math.cos(angle)
    sine_value = math.sin(angle)
    entries = []
    for number in range(8):
        signs = [1.0 if number >> bit & 1 else -1.0 for bit in range(3)]
        unit = np.array(signs) / math.sqrt(3.0)
        cross = np.array([[0.0, -unit[2], unit[1]], [unit[2], 0.0, -unit[0]], [-unit[1], unit[0], 0.0]])
        matrix = cosine * np.eye(3) + (1.0 - cosine) * np.outer(unit, unit) + sine_value * cross
        entries.append(matrix.reshape(9))
    return np.array(entries)

def cell_rotation(axis_ids, table):
    matrix = jnp.zeros((9,) + axis_ids.shape, jnp.float32)
    for number in range(8):
        chosen = jnp.where(axis_ids == number, 1.0, 0.0).astype(jnp.float32)
        matrix = matrix + chosen[None] * table[number].reshape((9,) + (1,) * axis_ids.ndim)
    return matrix

def apply_rotation(matrix, vector):
    rows = [matrix[3 * row] * vector[0] + matrix[3 * row + 1] * vector[1] + matrix[3 * row + 2] * vector[2] for row in range(3)]
    return jnp.stack(rows)

def reference(velocities, particle_cells, grid_shift, axis_index, migrate_dir, migrate_slot, contact_colloid, contact_particle, contact_weight, colloid_velocity):
    table = jnp.asarray(rotation_table(), jnp.float32)
    cell_total = NX * NY * NZ
    device = (jnp.arange(PARTICLES) // P_DEV).astype(jnp.int32)
    device_x = device // (N_GY * N_GZ)
    device_y = device // N_GZ % N_GY
    device_z = device % N_GZ
    velocity_now = velocities
    mean = jnp.zeros((3, cell_total), jnp.float32)
    for step in range(STEPS):
        local = particle_cells[step]
        cell_x = (device_x * CX + local // (CY * CZ) + grid_shift[step, 0]) % NX
        cell_y = (device_y * CY + local // CZ % CY + grid_shift[step, 1]) % NY
        cell_z = (device_z * CZ + local % CZ + grid_shift[step, 2]) % NZ
        cell = ((cell_x * NY + cell_y) * NZ + cell_z).astype(jnp.int32)
        momentum = jnp.zeros((3, cell_total), jnp.float32).at[:, cell].add(velocity_now)
        counts = jnp.zeros((cell_total,), jnp.float32).at[cell].add(1.0)
        mean = momentum / jnp.maximum(counts, 1.0)
        matrix = cell_rotation(axis_index[step].reshape(-1), table)
        offset = mean - apply_rotation(matrix, mean)
        velocity_now = apply_rotation(matrix[:, cell], velocity_now) + offset[:, cell]
    cell_velocity = mean.reshape(3, NX, NY, NZ)
    device_list = PARTICLES // P_DEV
    leaving = migrate_dir > 0
    target = jnp.where(leaving, device * (6 * CAP) + (migrate_dir - 1) * CAP + migrate_slot, device_list * 6 * CAP).astype(jnp.int32)
    outbox = jnp.zeros((3, device_list * 6 * CAP), jnp.float32).at[:, target].set(velocity_now, mode='drop')
    outbox = outbox.reshape(3, N_GX, N_GY, N_GZ, 6, CAP)
    moves = ((1, 1), (1, -1), (2, 1), (2, -1), (3, 1), (3, -1))
    arrivals = [jnp.roll(outbox[:, :, :, :, number, :], sign, axis=dim) for number, (dim, sign) in enumerate(moves)]
    arrivals = jnp.stack(arrivals, axis=4).reshape(3, device_list, 6 * CAP)
    kept = jnp.where(leaving[None], 0.0, velocity_now).reshape(3, device_list, P_DEV)
    migrated = jnp.concatenate([kept, arrivals], axis=2).reshape(3, device_list * (P_DEV + 6 * CAP))
    contact_device = (jnp.arange(CONTACTS) // CONTACTS_PER_UNIT).astype(jnp.int32)
    particle = (contact_device * P_DEV + contact_particle).astype(jnp.int32)
    weighted = contact_weight[None] * velocity_now[:, particle]
    sum_wv = jnp.zeros((3, COLLOIDS), jnp.float32).at[:, contact_colloid].add(weighted)
    sum_w = jnp.zeros((COLLOIDS,), jnp.float32).at[contact_colloid].add(contact_weight)
    colloid_force = (sum_wv - sum_w * colloid_velocity) / jnp.maximum(sum_w, 1.0)
    return (cell_velocity, migrated, colloid_force)
```

```python
import functools
import math

import jax
import jax.numpy as jnp
from jax import lax
from jax.experimental import pallas as pl
from jax.experimental.pallas import tpu as pltpu
from jax.sharding import PartitionSpec as P

CAP = 160
ANGLE = 130.0 * math.pi / 180.0
COS, SIN = math.cos(ANGLE), math.sin(ANGLE)
NT = (((1,), (1,)), ((), ()))
BF = jnp.bfloat16
F8 = jnp.float8_e4m3fn
F32 = jnp.float32
I32 = jnp.int32
HI, LO = 16, 256
PLANES = 10
PRE = 8.0
SLOT = 64
TOP = 1 << 19
AXES = ("gx", "gy", "gz")
MESH = pl.DeviceIdType.MESH


def split_index(c, low):
    if low & (low - 1) == 0:
        return c >> (low.bit_length() - 1), c & (low - 1)
    return c // low, c % low


def one():
    return jnp.ones((), BF)


def zero():
    return jnp.zeros((), BF)


def one_hot(row, count):
    kind = BF if count <= 256 else F32
    wide = lax.broadcasted_iota(I32, (count, row.shape[1]), 0).astype(F32).astype(kind)
    return jnp.where(wide == row.astype(F32).astype(kind), jnp.ones((), kind), jnp.zeros((), kind)).astype(BF)


def halves(x):
    high = x.astype(BF)
    return high, (x - high.astype(F32)).astype(BF)


def spread(rows, mask):
    return jnp.concatenate([mask * row for row in rows], axis=0)


def row_at(ref, plane, j, rows):
    return jnp.broadcast_to(ref[plane, j : j + 1], (rows, 128)).astype(BF)


def iotas(count):
    return [(lax.broadcasted_iota(I32, (16, 128), 0) + 16 * i).astype(F32).astype(BF) for i in range(count // 16)]


def pieces(x):
    x = x * PRE
    a = x.astype(F8).astype(F32)
    r = (x - a) * 16.0
    b = r.astype(F8).astype(F32)
    s = (r - b) * 16.0
    return a, b, s.astype(F8).astype(F32)


def stage_hist(st, cell, v):
    st[0] = ((cell & 127) | ((cell >> 11) << 7)).astype(F32)
    st[1] = ((cell >> 7) & 15).astype(F32)
    for k in range(3):
        for i, piece in enumerate(pieces(v[k])):
            st[2 + 3 * k + i] = piece


def hist_group(st, j, steps):
    low, high = row_at(st, 0, j, 16), row_at(st, 1, j, 16)
    hot = []
    for i in range(LO // 32):
        pair = [jnp.where(steps[2 * i + k] == low, one(), zero()) for k in range(2)]
        hot.append(jnp.concatenate(pair, axis=0).astype(F8))
    here = steps[0] == high
    rows = [jnp.where(here, row_at(st, 2 + q, j, 16), zero()) for q in range(PLANES - 1)]
    rows.append(jnp.where(here, one(), zero()))
    left = [jnp.concatenate(rows[2 * i : 2 * i + 2], axis=0).astype(F8) for i in range(PLANES // 2)]
    return jnp.concatenate(hot, axis=0), jnp.concatenate(left, axis=0)


def hist_add(acc, st, tiles, steps):
    groups = [hist_group(st.at[u], j, steps) for u in tiles for j in range(8)]
    left = jnp.concatenate([g[1] for g in groups], axis=1)
    hot = jnp.concatenate([g[0] for g in groups], axis=1)
    acc[...] += lax.dot_general(left, hot, NT, preferred_element_type=F32)


def mean_of(total, mean_ref):
    def plane(q):
        x = total[q * HI : (q + 1) * HI]
        return jnp.concatenate([x[:, :128], x[:, 128:]], axis=0)

    count = jnp.maximum(plane(9), 1.0)
    for k in range(3):
        sums = plane(3 * k) + plane(3 * k + 1) * (1.0 / 16) + plane(3 * k + 2) * (1.0 / 256)
        mean_ref[k] = sums * (1.0 / PRE) / count


def signs_of(index):
    return [jnp.where((index & (1 << i)) != 0, 1.0, -1.0) for i in range(3)]


def rotate(e, v):
    along = ((1.0 - COS) / 3.0) * (e[0] * v[0] + e[1] * v[1] + e[2] * v[2])
    turn = SIN / math.sqrt(3.0)
    out = []
    for i in range(3):
        j, k = (i + 1) % 3, (i + 2) % 3
        out.append(COS * v[i] + e[i] * along + turn * (e[j] * v[k] - e[k] * v[j]))
    return out


def make_table(mean_ref, axis_ref, table_ref, unit_ref):
    mean = [mean_ref[k] for k in range(3)]
    index = axis_ref[...]
    turned = rotate(signs_of(index), mean)
    offset = [mean[k] - turned[k] for k in range(3)]
    most = jnp.maximum(jnp.maximum(jnp.abs(offset[0]), jnp.abs(offset[1])), jnp.abs(offset[2]))
    most = jnp.max(jnp.max(most, axis=0, keepdims=True), axis=1, keepdims=True)
    most = jnp.maximum(most, 1e-25)
    scale = (TOP - 2.0) / most
    q = []
    for k in range(3):
        x = offset[k] * scale
        q.append((x + jnp.where(x >= 0.0, 0.5, -0.5)).astype(I32))
    last = q[2] + TOP
    table_ref[0] = (q[0] << 12) | (last >> 8)
    table_ref[1] = (q[1] << 12) | ((last & 255) << 4) | index
    unit_ref[...] = jnp.broadcast_to(most * (1.0 / (TOP - 2.0)), (8, 128))


def look_up(table_ref, cell):
    lane = cell & 127
    depth = table_ref.shape[1].bit_length() - 1
    bits = [(cell & (1 << (7 + b))) != 0 for b in range(depth)]

    def pick(word, b, at):
        if b < 0:
            row = jnp.broadcast_to(table_ref[word, at : at + 1], (8, 128))
            return jnp.take_along_axis(row, lane, axis=1, mode="promise_in_bounds")
        return jnp.where(bits[b], pick(word, b - 1, at + (1 << b)), pick(word, b - 1, at))

    return pick(0, depth - 1, 0), pick(1, depth - 1, 0)


def collide(table_ref, unit, cell, v):
    a, b = look_up(table_ref, cell)
    last = (((a & 4095) << 8) | ((b >> 4) & 255)) - TOP
    offset = [(x.astype(F32)) * unit for x in (a >> 12, b >> 12, last)]
    turned = rotate(signs_of(b), v)
    return [turned[k] + offset[k] for k in range(3)]


def beside(axis, sign):
    count = lax.axis_size(axis)
    return {axis: lax.rem(lax.axis_index(axis) + (sign + count), count)}


def greet():
    for axis in AXES:
        for sign in (1, -1):
            pl.semaphore_signal(
                pltpu.get_barrier_semaphore(), inc=1, device_id=beside(axis, sign), device_id_type=MESH
            )


def send(src, dst, sems, number, axis, sign):
    copy = pltpu.make_async_remote_copy(
        src_ref=src, dst_ref=dst, send_sem=sems[0].at[number], recv_sem=sems[1].at[number],
        device_id=beside(axis, sign), device_id_type=MESH,
    )
    copy.start()
    return copy


def both(pair, box, sems, number, axis):
    return [
        send(pair[0], box.at[0], sems, number, axis, -1),
        send(pair[1], box.at[1], sems, number + 1, axis, 1),
    ]


def shift_fields(rows, flip, shift_ref, x_ref, put, boxes, sems, first, before):
    zbox, xbox, ybox, work, turned, faces = boxes
    n, cx, cy, nz = x_ref.shape
    ups = [[shift_ref[r, dim] * flip > 0 for dim in range(3)] for r in rows]
    yield
    before()
    copies = both((x_ref, x_ref), zbox, sems, first, "gz")
    yield
    for copy in copies:
        copy.wait()
    for f in range(n):
        x = x_ref[f]
        plus = jnp.concatenate([x[:, :, 1:], zbox[0, f][:, :, 0:1]], axis=2)
        minus = jnp.concatenate([zbox[1, f][:, :, nz - 1 :], x[:, :, : nz - 1]], axis=2)
        work[f] = jnp.where(ups[f][2], plus, minus)
    copies = both((work.at[:, 0], work.at[:, cx - 1]), xbox, sems, first + 2, "gx")
    yield
    for copy in copies:
        copy.wait()
    for f in range(n):
        for i in range(cx):
            plus = work[f, i + 1] if i + 1 < cx else xbox[0, f]
            minus = work[f, i - 1] if i > 0 else xbox[1, f]
            row = jnp.where(ups[f][0], plus, minus)
            turned[f, i] = row
            faces[0, f, i : i + 1, :] = row[0:1]
            faces[1, f, i : i + 1, :] = row[cy - 1 :]
    copies = both((faces.at[0], faces.at[1]), ybox, sems, first + 4, "gy")
    yield
    for copy in copies:
        copy.wait()
    for f in range(n):
        for i in range(cx):
            x = turned[f, i]
            plus = jnp.concatenate([x[1:], ybox[0, f, i : i + 1, :]], axis=0)
            minus = jnp.concatenate([ybox[1, f, i : i + 1, :], x[: cy - 1]], axis=0)
            put(f, i, jnp.where(ups[f][1], plus, minus))


def shift_scratch(shape, kind):
    n, cx, cy, nz = shape
    return [
        pltpu.VMEM((2, n, cx, cy, nz), kind), pltpu.VMEM((2, n, cy, nz), kind),
        pltpu.VMEM((2, n, cx, nz), kind), pltpu.VMEM((n, cx, cy, nz), kind),
        pltpu.VMEM((n, cx, cy, nz), kind), pltpu.VMEM((2, n, cx, nz), kind),
    ]


def beside_work(transfer, step, count):
    for part in range(4):
        next(transfer)
        lax.fori_loop(count * part // 4, count * (part + 1) // 4, step, 0)
    for _ in transfer:
        pass


def contact_places(colloid, units):
    size_x, size_y, size_z = (lax.axis_size(a) for a in AXES)
    mine_x, mine_y, mine_z = (lax.axis_index(a) for a in AXES)
    owner, member = split_index(colloid, units)
    rest, own_z = split_index(owner, size_z)
    own_x, own_y = split_index(rest, size_y)

    def apart(own, mine, size):
        return split_index(own - mine + size, size)[1]

    apart_x, apart_y, apart_z = apart(own_x, mine_x, size_x), apart(own_y, mine_y, size_y), apart(own_z, mine_z, size_z)
    code = jnp.full(colloid.shape, 6, I32)
    pairs = (
        (apart_x, 1), (apart_x, size_x - 1), (apart_y, 1),
        (apart_y, size_y - 1), (apart_z, 1), (apart_z, size_z - 1),
    )
    for number, (gap, to) in reversed(list(enumerate(pairs))):
        code = jnp.where(gap == to, number, code)
    return code, member


def main_kernel(
    per, units, shift_ref, v_in, cs, axis_hbm, dir_hbm, slot_hbm, who_hbm, colloid_hbm, weight_hbm, drift_ref,
    kept_ref, tail_ref, cellv_ref, force_ref,
    vs, field, dirs, slots, who, colloid, weight, axes, mean, field_mean, table, unit_ref, st, acc, moved, book,
    going, coming, pushes, pulls, *rest
):
    boxes_a, boxes_b, (local_sem, out_sem, in_sem) = rest[:6], rest[6:12], rest[12:]
    sems = (out_sem, in_sem)
    cx, cy, nz = axis_hbm.shape[1:]
    groups = v_in.shape[1]
    loops = groups // (8 * per)

    def fetch(src, dst, number):
        copy = pltpu.make_async_copy(src, dst, local_sem.at[number])
        copy.start()
        return copy

    first = [fetch(axis_hbm, field, 0)]
    late = [fetch(dir_hbm, dirs, 1), fetch(slot_hbm, slots, 2), fetch(who_hbm, who, 3)]
    late += [fetch(colloid_hbm, colloid, 4), fetch(weight_hbm, weight, 5)]
    greet()

    steps = iotas(LO)

    def rows_of(t, u):
        return pl.ds(pl.multiple_of((t * per + u) * 8, 8), 8)

    def meet():
        pl.semaphore_wait(pltpu.get_barrier_semaphore(), 6)
        first[0].wait()

    def put_axis(f, i, value):
        axes[f, i * cy : (i + 1) * cy, :] = value

    acc[...] = jnp.zeros_like(acc)

    def step0(t, carry):
        for u in range(per):
            at = rows_of(t, u)
            stage_hist(st.at[u], cs[0, at], [v_in[k, at] for k in range(3)])
        hist_add(acc, st, range(per), steps)
        return carry

    transfer = shift_fields((0, 1), 1, shift_ref, field, put_axis, boxes_a, sems, 0, meet)
    beside_work(transfer, step0, loops)
    mean_of(acc[...], mean)
    for copy in late:
        copy.wait()
    make_table(mean, axes.at[0], table, unit_ref)
    acc[...] = jnp.zeros_like(acc)

    def step1(t, carry):
        unit = unit_ref[...]
        for u in range(per):
            at = rows_of(t, u)
            new = collide(table, unit, cs[0, at], [v_in[k, at] for k in range(3)])
            for k in range(3):
                vs[k, at] = new[k]
            stage_hist(st.at[u], cs[1, at], new)
        hist_add(acc, st, range(per), steps)
        return carry

    lax.fori_loop(0, loops, step1, 0)
    mean_of(acc[...], mean)
    make_table(mean, axes.at[1], table, unit_ref)
    for k in range(3):
        for i in range(cx):
            field_mean[k, i] = mean[k, i * cy : (i + 1) * cy]
    moved[...] = jnp.zeros_like(moved)
    narrow = iotas(SLOT)

    def leave_group(ref, j):
        low, high = row_at(ref, 0, j, 16), row_at(ref, 1, j, 16)
        hot = jnp.concatenate([jnp.where(wide == low, one(), zero()) for wide in narrow], axis=0)
        here = narrow[0] == high
        rows = [jnp.where(here, row_at(ref, 2 + q, j, 16), zero()) for q in range(6)]
        return hot, jnp.concatenate(rows, axis=0)

    def step2(t, carry):
        unit = unit_ref[...]
        hots, lefts = [], []
        for u in range(per):
            at = rows_of(t, u)
            new = collide(table, unit, cs[1, at], [vs[k, at] for k in range(3)])
            code = dirs[at]
            stays = code == 0
            goal = jnp.where(stays, -SLOT, (code - 1) * CAP + slots[at])
            st[u, 0] = (goal & (SLOT - 1)).astype(F32)
            st[u, 1] = (goal >> (SLOT.bit_length() - 1)).astype(F32)
            for k in range(3):
                kept_ref[k, at] = jnp.where(stays, new[k], 0.0)
                high, low = halves(new[k])
                st[u, 2 + 2 * k] = high.astype(F32)
                st[u, 3 + 2 * k] = low.astype(F32)
        for u in range(0, per, 2):
            at = pl.ds(pl.multiple_of((t * per + u) * 8, 16), 16)
            for k in range(3):
                for i in range(2):
                    both_tiles = jnp.concatenate([st[u, 2 + 2 * k + i], st[u + 1, 2 + 2 * k + i]], axis=0)
                    book[k, at, i * 128 : (i + 1) * 128] = both_tiles.astype(BF)
        for u in range(per):
            for j in range(8):
                hot, left = leave_group(st.at[u], j)
                hots.append(hot)
                lefts.append(left)
        moved[...] += lax.dot_general(
            jnp.concatenate(lefts, axis=1), jnp.concatenate(hots, axis=1), NT, preferred_element_type=F32
        )
        return carry

    def put_mean(f, i, value):
        cellv_ref[f, i] = value

    rows_of_shift = [shift_ref.shape[0] - 1] * 3
    transfer = shift_fields(
        rows_of_shift, -1, shift_ref, field_mean, put_mean, boxes_b, sems, 6, lambda: None
    )
    beside_work(transfer, step2, loops)

    for k in range(3):
        value = moved[32 * k : 32 * k + 16] + moved[32 * k + 16 : 32 * k + 32]
        for d in range(6):
            at, end, parts = d * CAP, (d + 1) * CAP, []
            while at < end:
                r, c = at // SLOT, at % SLOT
                size = min(SLOT - c, end - at)
                parts.append(value[r : r + 1, c : c + size])
                at += size
            going[d, k : k + 1, :] = jnp.concatenate(parts, axis=1)
    copies = [
        send(going.at[d], coming.at[d], sems, 12 + d, AXES[d // 2], 1 - 2 * (d % 2)) for d in range(6)
    ]

    contacts = who.shape[1]
    chunk = min(512, contacts)
    sums = jnp.zeros((8 * 16, units), F32)
    pages = book[...].reshape(3 * groups, 256)
    for c in range(contacts // chunk):
        at = slice(c * chunk, (c + 1) * chunk)
        hi, lo = split_index(who[0:1, at], 128)
        hot = one_hot(lo, 128)
        got = jnp.dot(pages, jnp.concatenate([hot, hot], axis=0), preferred_element_type=F32)
        here = lax.broadcasted_iota(I32, (groups, chunk), 0) == hi
        force = weight[0:1, at]
        rows = []
        for k in range(3):
            mine = jnp.where(here, got[k * groups : (k + 1) * groups], 0.0)
            rows.extend(halves(force * jnp.sum(mine, axis=0, keepdims=True)))
        rows.extend(halves(force))
        code, member = contact_places(colloid[0:1, at], units)
        sums = sums + lax.dot_general(
            spread(rows, one_hot(code, 16)), one_hot(member, units), NT, preferred_element_type=F32
        )
    totals = [sums[32 * k : 32 * k + 16] + sums[32 * k + 16 : 32 * k + 32] for k in range(4)]
    total = jnp.concatenate([x[6:7] for x in totals], axis=0)
    for d in range(6):
        for k in range(4):
            pushes[d, k : k + 1, :] = totals[k][d : d + 1]
    more = [
        send(pushes.at[d], pulls.at[d], sems, 18 + d, AXES[d // 2], 1 - 2 * (d % 2)) for d in range(6)
    ]
    for d, copy in enumerate(copies):
        copy.wait()
        for k in range(3):
            tail_ref[k, :, d * CAP : (d + 1) * CAP] = coming[d, k : k + 1]
    for d, copy in enumerate(more):
        copy.wait()
        total = total + pulls[d]
    sum_w = total[3:4]
    force_ref[...] = (total[0:3] - sum_w * drift_ref[...]) / jnp.maximum(sum_w, 1.0)


def last_kernel(kept_ref, tail_ref, cellv_ref, force_ref, cellv_hbm, out_hbm, force_hbm, sem):
    particles, extra = kept_ref.shape[2], tail_ref.shape[2]
    copies = []
    for k in range(3):
        row = pl.ds(k, 1)
        copies.append((kept_ref.at[k], out_hbm.at[row, pl.ds(0, particles)]))
        copies.append((tail_ref.at[k], out_hbm.at[row, pl.ds(particles, extra)]))
    copies += [(cellv_ref, cellv_hbm), (force_ref, force_hbm)]
    copies = [pltpu.make_async_copy(src, dst, sem.at[i]) for i, (src, dst) in enumerate(copies)]
    for copy in copies:
        copy.start()
    for copy in copies:
        copy.wait()


def body(
    velocities, particle_cells, grid_shift, axis_index, migrate_dir, migrate_slot,
    contact_colloid, contact_particle, contact_weight, colloid_velocity,
):
    _, cx, cy, nlo = axis_index.shape
    particles = velocities.shape[1]
    units = colloid_velocity.shape[1]
    contacts = contact_weight.shape[0]
    groups = particles // 128
    cells = (cx * cy, nlo)
    if cells != (2 * HI, 128) or particles % 4096 or 6 * CAP > 16 * SLOT:
        raise ValueError("sizes")
    per = 4
    grid_mean = (3, cx, cy, nlo)
    vmem = pl.BlockSpec(memory_space=pltpu.VMEM)
    smem = pl.BlockSpec(memory_space=pltpu.SMEM)
    hbm = pl.BlockSpec(memory_space=pl.ANY)
    outs = (
        jax.ShapeDtypeStruct((3, groups, 128), F32),
        jax.ShapeDtypeStruct((3, 1, 6 * CAP), F32),
        jax.ShapeDtypeStruct(grid_mean, F32),
        jax.ShapeDtypeStruct((3, units), F32),
    )
    dma = pltpu.SemaphoreType.DMA
    kept, tail, cellv, force = pl.pallas_call(
        functools.partial(main_kernel, per, units),
        out_shape=outs,
        in_specs=[smem] + [vmem] * 2 + [hbm] * 6 + [vmem],
        out_specs=(vmem,) * 4,
        scratch_shapes=[
            pltpu.VMEM((3, groups, 128), F32), pltpu.VMEM(axis_index.shape, I32), pltpu.VMEM((groups, 128), I32), pltpu.VMEM((groups, 128), I32),
            pltpu.VMEM((1, contacts), I32), pltpu.VMEM((1, contacts), I32), pltpu.VMEM((1, contacts), F32),
            pltpu.VMEM((2,) + cells, I32), pltpu.VMEM((3,) + cells, F32), pltpu.VMEM(grid_mean, F32),
            pltpu.VMEM((2,) + cells, I32), pltpu.VMEM((8, 128), F32), pltpu.VMEM((per, PLANES + 1, 8, 128), F32),
            pltpu.VMEM((PLANES * HI, LO), F32), pltpu.VMEM((96, SLOT), F32), pltpu.VMEM((3, groups, 256), BF),
            pltpu.VMEM((6, 3, CAP), F32), pltpu.VMEM((6, 3, CAP), F32),
            pltpu.VMEM((6, 4, units), F32), pltpu.VMEM((6, 4, units), F32),
        ]
        + shift_scratch(axis_index.shape, I32) + shift_scratch(grid_mean, F32)
        + [dma((6,)), dma((24,)), dma((24,))],
        compiler_params=pltpu.CompilerParams(
            vmem_limit_bytes=48 * 2**20, collective_id=0, has_side_effects=True
        ),
        cost_estimate=pl.CostEstimate(flops=10**9, bytes_accessed=30_000_000, transcendentals=0),
    )(
        grid_shift, velocities.reshape(3, groups, 128), particle_cells.reshape(2, groups, 128), axis_index, migrate_dir.reshape(groups, 128),
        migrate_slot.reshape(groups, 128), contact_particle.reshape(1, -1), contact_colloid.reshape(1, -1),
        contact_weight.reshape(1, -1), colloid_velocity,
    )
    return pl.pallas_call(
        last_kernel,
        out_shape=(
            jax.ShapeDtypeStruct(grid_mean, F32),
            jax.ShapeDtypeStruct((3, particles + 6 * CAP), F32),
            jax.ShapeDtypeStruct((3, units), F32),
        ),
        in_specs=[vmem] * 4,
        out_specs=(hbm,) * 3,
        scratch_shapes=[dma((8,))],
        compiler_params=pltpu.CompilerParams(vmem_limit_bytes=8 * 2**20),
    )(kept.reshape(3, 1, particles), tail, cellv, force)


def solution(mesh):
    flat = P(None, AXES)
    line = P(AXES)
    grid = P(None, *AXES)

    return jax.shard_map(
        body,
        mesh=mesh,
        in_specs=(flat, flat, P(), grid, line, line, line, line, line, flat),
        out_specs=(grid, flat, flat),
        check_vma=False,
    )
```

```python
import functools
import math

import jax
import jax.numpy as jnp
from jax import lax
from jax.experimental import pallas as pl
from jax.experimental.pallas import tpu as pltpu
from jax.sharding import PartitionSpec as P

CAP = 160
ANGLE = 130.0 * math.pi / 180.0
COS, SIN = math.cos(ANGLE), math.sin(ANGLE)
NT = (((1,), (1,)), ((), ()))
BF = jnp.bfloat16
F8 = jnp.float8_e4m3fn
F32 = jnp.float32
I32 = jnp.int32
HI, LO = 16, 256
PLANES = 10
PRE = 8.0
SLOT = 64
TOP = 1 << 19
EARLY = 1
AXES = ("gx", "gy", "gz")
MESH = pl.DeviceIdType.MESH
WAYS = [(x, y, z) for x in (-1, 0, 1) for y in (-1, 0, 1) for z in (-1, 0, 1) if (x, y, z) != (0, 0, 0)]


def split_index(c, low):
    if low & (low - 1) == 0:
        return c >> (low.bit_length() - 1), c & (low - 1)
    return c // low, c % low


def one():
    return jnp.ones((), BF)


def zero():
    return jnp.zeros((), BF)


def one_hot(row, count):
    kind = BF if count <= 256 else F32
    wide = lax.broadcasted_iota(I32, (count, row.shape[1]), 0).astype(F32).astype(kind)
    return jnp.where(wide == row.astype(F32).astype(kind), jnp.ones((), kind), jnp.zeros((), kind)).astype(BF)


def halves(x):
    high = x.astype(BF)
    return high, (x - high.astype(F32)).astype(BF)


def spread(rows, mask):
    return jnp.concatenate([mask * row for row in rows], axis=0)


def row_at(ref, plane, j, rows):
    return jnp.broadcast_to(ref[plane, j : j + 1], (rows, 128)).astype(BF)


def iotas(count):
    return [(lax.broadcasted_iota(I32, (16, 128), 0) + 16 * i).astype(F32).astype(BF) for i in range(count // 16)]


def pieces(x):
    x = x * PRE
    a = x.astype(F8).astype(F32)
    r = (x - a) * 16.0
    b = r.astype(F8).astype(F32)
    s = (r - b) * 16.0
    return a, b, s.astype(F8).astype(F32)


def stage_hist(st, cell, v):
    st[0] = ((cell & 127) | ((cell >> 11) << 7)).astype(F32)
    st[1] = ((cell >> 7) & 15).astype(F32)
    for k in range(3):
        for i, piece in enumerate(pieces(v[k])):
            st[2 + 3 * k + i] = piece


def hist_group(st, j, steps):
    low, high = row_at(st, 0, j, 16), row_at(st, 1, j, 16)
    hot = []
    for i in range(LO // 32):
        pair = [jnp.where(steps[2 * i + k] == low, one(), zero()) for k in range(2)]
        hot.append(jnp.concatenate(pair, axis=0).astype(F8))
    here = steps[0] == high
    rows = [jnp.where(here, row_at(st, 2 + q, j, 16), zero()) for q in range(PLANES - 1)]
    rows.append(jnp.where(here, one(), zero()))
    left = [jnp.concatenate(rows[2 * i : 2 * i + 2], axis=0).astype(F8) for i in range(PLANES // 2)]
    return jnp.concatenate(hot, axis=0), jnp.concatenate(left, axis=0)


def hist_add(acc, st, tiles, steps):
    groups = [hist_group(st.at[u], j, steps) for u in tiles for j in range(8)]
    left = jnp.concatenate([g[1] for g in groups], axis=1)
    hot = jnp.concatenate([g[0] for g in groups], axis=1)
    acc[...] += lax.dot_general(left, hot, NT, preferred_element_type=F32)


def mean_of(total, mean_ref):
    def plane(q):
        x = total[q * HI : (q + 1) * HI]
        return jnp.concatenate([x[:, :128], x[:, 128:]], axis=0)

    count = jnp.maximum(plane(9), 1.0)
    for k in range(3):
        sums = plane(3 * k) + plane(3 * k + 1) * (1.0 / 16) + plane(3 * k + 2) * (1.0 / 256)
        mean_ref[k] = sums * (1.0 / PRE) / count


def signs_of(index):
    return [jnp.where((index & (1 << i)) != 0, 1.0, -1.0) for i in range(3)]


def rotate(e, v):
    along = ((1.0 - COS) / 3.0) * (e[0] * v[0] + e[1] * v[1] + e[2] * v[2])
    turn = SIN / math.sqrt(3.0)
    out = []
    for i in range(3):
        j, k = (i + 1) % 3, (i + 2) % 3
        out.append(COS * v[i] + e[i] * along + turn * (e[j] * v[k] - e[k] * v[j]))
    return out


def make_table(mean_ref, axis_ref, table_ref, unit_ref):
    mean = [mean_ref[k] for k in range(3)]
    index = axis_ref[...]
    turned = rotate(signs_of(index), mean)
    offset = [mean[k] - turned[k] for k in range(3)]
    most = jnp.maximum(jnp.maximum(jnp.abs(offset[0]), jnp.abs(offset[1])), jnp.abs(offset[2]))
    most = jnp.max(jnp.max(most, axis=0, keepdims=True), axis=1, keepdims=True)
    most = jnp.maximum(most, 1e-25)
    scale = (TOP - 2.0) / most
    q = []
    for k in range(3):
        x = offset[k] * scale
        q.append((x + jnp.where(x >= 0.0, 0.5, -0.5)).astype(I32))
    last = q[2] + TOP
    table_ref[0] = (q[0] << 12) | (last >> 8)
    table_ref[1] = (q[1] << 12) | ((last & 255) << 4) | index
    unit_ref[...] = jnp.broadcast_to(most * (1.0 / (TOP - 2.0)), (8, 128))


def look_up(table_ref, cell):
    lane = cell & 127
    depth = table_ref.shape[1].bit_length() - 1
    bits = [(cell & (1 << (7 + b))) != 0 for b in range(depth)]

    def pick(word, b, at):
        if b < 0:
            row = jnp.broadcast_to(table_ref[word, at : at + 1], (8, 128))
            return jnp.take_along_axis(row, lane, axis=1, mode="promise_in_bounds")
        return jnp.where(bits[b], pick(word, b - 1, at + (1 << b)), pick(word, b - 1, at))

    return pick(0, depth - 1, 0), pick(1, depth - 1, 0)


def collide(table_ref, unit, cell, v):
    a, b = look_up(table_ref, cell)
    last = (((a & 4095) << 8) | ((b >> 4) & 255)) - TOP
    offset = [(x.astype(F32)) * unit for x in (a >> 12, b >> 12, last)]
    turned = rotate(signs_of(b), v)
    return [turned[k] + offset[k] for k in range(3)]


def beside(axis, sign):
    count = lax.axis_size(axis)
    return {axis: lax.rem(lax.axis_index(axis) + (sign + count), count)}


def kept_ways():
    return [w for w in WAYS if w[2] >= 0 or lax.axis_size("gz") > 2]


def greet():
    for way in kept_ways():
        pl.semaphore_signal(
            pltpu.get_barrier_semaphore(), inc=1, device_id=towards(way), device_id_type=MESH
        )


def towards(way):
    target = {}
    for axis, sign in zip(AXES, way):
        if sign:
            target.update(beside(axis, sign))
    return target


def send(src, dst, sems, number, axis, sign):
    copy = pltpu.make_async_remote_copy(
        src_ref=src, dst_ref=dst, send_sem=sems[0].at[number], recv_sem=sems[1].at[number],
        device_id=beside(axis, sign), device_id_type=MESH,
    )
    copy.start()
    return copy


def start_shift(x_ref, boxes, sems, first):
    zbox, xbox, ybox, faces = boxes
    n, cx, cy, _ = x_ref.shape
    for f in range(n):
        for i in range(cx):
            faces[0, f, i : i + 1, :] = x_ref[f, i, 0:1]
            faces[1, f, i : i + 1, :] = x_ref[f, i, cy - 1 : cy]
    copies = []
    for number, way in enumerate(kept_ways()):
        x, y, z = way
        if y:
            src, dst = faces.at[0 if y > 0 else 1], ybox.at[x + 1, 0 if y > 0 else 1, z + 1]
        elif x:
            src, dst = x_ref.at[:, 0 if x > 0 else cx - 1], xbox.at[0 if x > 0 else 1, z + 1]
        else:
            src, dst = x_ref, zbox.at[0 if z > 0 else 1]
        copy = pltpu.make_async_remote_copy(
            src_ref=src, dst_ref=dst, send_sem=sems[0].at[first + number], recv_sem=sems[1].at[first + number],
            device_id=towards((-x, -y, -z)), device_id_type=MESH,
        )
        copy.start()
        copies.append(copy)
    return copies


def finish_shift(copies, rows, flip, shift_ref, x_ref, boxes, put):
    zbox, xbox, ybox, _ = boxes
    n, cx, cy, nz = x_ref.shape
    deep = lax.axis_size("gz") > 2
    levels = (0, 1, 2) if deep else (2, 1, 2)
    for copy in copies:
        copy.wait()
    for f in range(n):
        up_x, up_y, up_z = (shift_ref[rows[f], dim] * flip > 0 for dim in range(3))

        def turn(parts):
            low, mid, high = parts
            end = mid.ndim - 1
            cut = lambda v, at, to: lax.slice_in_dim(v, at, to, axis=end)
            plus = jnp.concatenate([cut(mid, 1, nz), cut(high, 0, 1)], axis=end)
            minus = jnp.concatenate([cut(low, nz - 1, nz), cut(mid, 0, nz - 1)], axis=end)
            return jnp.where(up_z, plus, minus)

        def edge(z):
            pick = [
                jnp.where(up_x, ybox[2, s, z, f, 0:1], ybox[0, s, z, f, cx - 1 : cx]) for s in range(2)
            ]
            return jnp.where(up_y, pick[0], pick[1])

        core = turn([zbox[1 if deep else 0, f], x_ref[f], zbox[0, f]])
        side = turn([jnp.where(up_x, xbox[0, z, f], xbox[1, z, f]) for z in levels])
        face = turn([jnp.where(up_y, ybox[1, 0, z, f], ybox[1, 1, z, f]) for z in levels])
        corner = turn([edge(z) for z in levels])
        for i in range(cx):
            plus = core[i + 1] if i + 1 < cx else side
            minus = core[i - 1] if i > 0 else side
            x = jnp.where(up_x, plus, minus)
            plus = face[i + 1 : i + 2] if i + 1 < cx else corner
            minus = face[i - 1 : i] if i > 0 else corner
            row = jnp.where(up_x, plus, minus)
            plus = jnp.concatenate([x[1:], row], axis=0)
            minus = jnp.concatenate([row, x[: cy - 1]], axis=0)
            put(f, i, jnp.where(up_y, plus, minus))


def shift_scratch(shape, kind):
    n, cx, cy, nz = shape
    return [
        pltpu.VMEM((2, n, cx, cy, nz), kind), pltpu.VMEM((2, 3, n, cy, nz), kind),
        pltpu.VMEM((3, 2, 3, n, cx, nz), kind), pltpu.VMEM((2, n, cx, nz), kind),
    ]


def contact_places(colloid, units):
    size_x, size_y, size_z = (lax.axis_size(a) for a in AXES)
    mine_x, mine_y, mine_z = (lax.axis_index(a) for a in AXES)
    owner, member = split_index(colloid, units)
    rest, own_z = split_index(owner, size_z)
    own_x, own_y = split_index(rest, size_y)

    def apart(own, mine, size):
        return split_index(own - mine + size, size)[1]

    apart_x, apart_y, apart_z = apart(own_x, mine_x, size_x), apart(own_y, mine_y, size_y), apart(own_z, mine_z, size_z)
    code = jnp.full(colloid.shape, 6, I32)
    pairs = (
        (apart_x, 1), (apart_x, size_x - 1), (apart_y, 1),
        (apart_y, size_y - 1), (apart_z, 1), (apart_z, size_z - 1),
    )
    for number, (gap, to) in reversed(list(enumerate(pairs))):
        code = jnp.where(gap == to, number, code)
    return code, member


def main_kernel(
    per, units, shift_hbm, v_in, cs, axis_hbm, dir_hbm, slot_hbm, who_hbm, colloid_hbm, weight_hbm, drift_hbm,
    kept_ref, tail_ref, cellv_ref, force_ref,
    vs, shift_ref, drift_ref, field, dirs, slots, who, colloid, weight, axes, mean, field_mean, table, unit_ref, st, acc, moved, book,
    going, coming, pushes, pulls, *rest
):
    boxes_a, boxes_b, (local_sem, out_sem, in_sem) = rest[:4], rest[4:8], rest[8:]
    sems = (out_sem, in_sem)
    cx, cy, nz = axis_hbm.shape[1:]
    groups = v_in.shape[1]
    loops = groups // (8 * per)

    def fetch(src, dst, number):
        copy = pltpu.make_async_copy(src, dst, local_sem.at[number])
        copy.start()
        return copy

    first = [fetch(axis_hbm, field, 0), fetch(shift_hbm, shift_ref, 7)]
    late = [fetch(dir_hbm, dirs, 1), fetch(slot_hbm, slots, 2), fetch(who_hbm, who, 3)]
    late += [fetch(colloid_hbm, colloid, 4), fetch(weight_hbm, weight, 5), fetch(drift_hbm, drift_ref, 6)]
    greet()

    steps = iotas(LO)

    def rows_of(t, u):
        return pl.ds(pl.multiple_of((t * per + u) * 8, 8), 8)

    def put_axis(f, i, value):
        axes[f, i * cy : (i + 1) * cy, :] = value

    acc[...] = jnp.zeros_like(acc)

    def step0(t, carry):
        for u in range(per):
            at = rows_of(t, u)
            stage_hist(st.at[u], cs[0, at], [v_in[k, at] for k in range(3)])
        hist_add(acc, st, range(per), steps)
        return carry

    lax.fori_loop(0, EARLY, step0, 0)
    pl.semaphore_wait(pltpu.get_barrier_semaphore(), len(kept_ways()))
    for copy in first:
        copy.wait()
    copies = start_shift(field, boxes_a, sems, 0)
    lax.fori_loop(EARLY, loops, step0, 0)
    finish_shift(copies, (0, 1), 1, shift_ref, field, boxes_a, put_axis)
    mean_of(acc[...], mean)
    for copy in late:
        copy.wait()
    make_table(mean, axes.at[0], table, unit_ref)
    acc[...] = jnp.zeros_like(acc)

    def step1(t, carry):
        unit = unit_ref[...]
        for u in range(per):
            at = rows_of(t, u)
            new = collide(table, unit, cs[0, at], [v_in[k, at] for k in range(3)])
            for k in range(3):
                vs[k, at] = new[k]
            stage_hist(st.at[u], cs[1, at], new)
        hist_add(acc, st, range(per), steps)
        return carry

    lax.fori_loop(0, loops, step1, 0)
    mean_of(acc[...], mean)
    make_table(mean, axes.at[1], table, unit_ref)
    for k in range(3):
        for i in range(cx):
            field_mean[k, i] = mean[k, i * cy : (i + 1) * cy]
    moved[...] = jnp.zeros_like(moved)
    narrow = iotas(SLOT)

    def leave_group(ref, j):
        low, high = row_at(ref, 0, j, 16), row_at(ref, 1, j, 16)
        hot = jnp.concatenate([jnp.where(wide == low, one(), zero()) for wide in narrow], axis=0)
        here = narrow[0] == high
        rows = [jnp.where(here, row_at(ref, 2 + q, j, 16), zero()) for q in range(6)]
        return hot, jnp.concatenate(rows, axis=0)

    def step2(t, carry):
        unit = unit_ref[...]
        hots, lefts = [], []
        for u in range(per):
            at = rows_of(t, u)
            new = collide(table, unit, cs[1, at], [vs[k, at] for k in range(3)])
            code = dirs[at]
            stays = code == 0
            goal = jnp.where(stays, -SLOT, (code - 1) * CAP + slots[at])
            st[u, 0] = (goal & (SLOT - 1)).astype(F32)
            st[u, 1] = (goal >> (SLOT.bit_length() - 1)).astype(F32)
            for k in range(3):
                kept_ref[k, at] = jnp.where(stays, new[k], 0.0)
                high, low = halves(new[k])
                st[u, 2 + 2 * k] = high.astype(F32)
                st[u, 3 + 2 * k] = low.astype(F32)
        for u in range(0, per, 2):
            at = pl.ds(pl.multiple_of((t * per + u) * 8, 16), 16)
            for k in range(3):
                for i in range(2):
                    both_tiles = jnp.concatenate([st[u, 2 + 2 * k + i], st[u + 1, 2 + 2 * k + i]], axis=0)
                    book[k, at, i * 128 : (i + 1) * 128] = both_tiles.astype(BF)
        for u in range(per):
            for j in range(8):
                hot, left = leave_group(st.at[u], j)
                hots.append(hot)
                lefts.append(left)
        moved[...] += lax.dot_general(
            jnp.concatenate(lefts, axis=1), jnp.concatenate(hots, axis=1), NT, preferred_element_type=F32
        )
        return carry

    def put_mean(f, i, value):
        cellv_ref[f, i] = value

    rows_of_shift = [shift_ref.shape[0] - 1] * 3
    means = start_shift(field_mean, boxes_b, sems, 26)
    lax.fori_loop(0, loops, step2, 0)

    for k in range(3):
        value = moved[32 * k : 32 * k + 16] + moved[32 * k + 16 : 32 * k + 32]
        for d in range(6):
            at, end, parts = d * CAP, (d + 1) * CAP, []
            while at < end:
                r, c = at // SLOT, at % SLOT
                size = min(SLOT - c, end - at)
                parts.append(value[r : r + 1, c : c + size])
                at += size
            going[d, k : k + 1, :] = jnp.concatenate(parts, axis=1)
    copies = [
        send(going.at[d], coming.at[d], sems, 52 + d, AXES[d // 2], 1 - 2 * (d % 2)) for d in range(6)
    ]

    contacts = who.shape[1]
    chunk = min(512, contacts)
    sums = jnp.zeros((8 * 16, units), F32)
    pages = book[...].reshape(3 * groups, 256)
    for c in range(contacts // chunk):
        at = slice(c * chunk, (c + 1) * chunk)
        hi, lo = split_index(who[0:1, at], 128)
        hot = one_hot(lo, 128)
        got = jnp.dot(pages, jnp.concatenate([hot, hot], axis=0), preferred_element_type=F32)
        here = lax.broadcasted_iota(I32, (groups, chunk), 0) == hi
        force = weight[0:1, at]
        rows = []
        for k in range(3):
            mine = jnp.where(here, got[k * groups : (k + 1) * groups], 0.0)
            rows.extend(halves(force * jnp.sum(mine, axis=0, keepdims=True)))
        rows.extend(halves(force))
        code, member = contact_places(colloid[0:1, at], units)
        sums = sums + lax.dot_general(
            spread(rows, one_hot(code, 16)), one_hot(member, units), NT, preferred_element_type=F32
        )
    totals = [sums[32 * k : 32 * k + 16] + sums[32 * k + 16 : 32 * k + 32] for k in range(4)]
    total = jnp.concatenate([x[6:7] for x in totals], axis=0)
    for d in range(6):
        for k in range(4):
            pushes[d, k : k + 1, :] = totals[k][d : d + 1]
    more = [
        send(pushes.at[d], pulls.at[d], sems, 58 + d, AXES[d // 2], 1 - 2 * (d % 2)) for d in range(6)
    ]
    finish_shift(means, rows_of_shift, -1, shift_ref, field_mean, boxes_b, put_mean)
    for d, copy in enumerate(copies):
        copy.wait()
        for k in range(3):
            tail_ref[k, :, d * CAP : (d + 1) * CAP] = coming[d, k : k + 1]
    for d, copy in enumerate(more):
        copy.wait()
        total = total + pulls[d]
    sum_w = total[3:4]
    force_ref[...] = (total[0:3] - sum_w * drift_ref[...]) / jnp.maximum(sum_w, 1.0)


def last_kernel(kept_ref, tail_ref, cellv_ref, force_ref, cellv_hbm, out_hbm, force_hbm, sem):
    particles, extra = kept_ref.shape[2], tail_ref.shape[2]
    copies = []
    for k in range(3):
        row = pl.ds(k, 1)
        copies.append((kept_ref.at[k], out_hbm.at[row, pl.ds(0, particles)]))
        copies.append((tail_ref.at[k], out_hbm.at[row, pl.ds(particles, extra)]))
    copies += [(cellv_ref, cellv_hbm), (force_ref, force_hbm)]
    copies = [pltpu.make_async_copy(src, dst, sem.at[i]) for i, (src, dst) in enumerate(copies)]
    for copy in copies:
        copy.start()
    for copy in copies:
        copy.wait()


def body(
    velocities, particle_cells, grid_shift, axis_index, migrate_dir, migrate_slot,
    contact_colloid, contact_particle, contact_weight, colloid_velocity,
):
    _, cx, cy, nlo = axis_index.shape
    particles = velocities.shape[1]
    units = colloid_velocity.shape[1]
    contacts = contact_weight.shape[0]
    groups = particles // 128
    cells = (cx * cy, nlo)
    if cells != (2 * HI, 128) or particles % 4096 or 6 * CAP > 16 * SLOT:
        raise ValueError("sizes")
    per = next(p for p in (8, 4) if groups % (8 * p) == 0)
    grid_mean = (3, cx, cy, nlo)
    vmem = pl.BlockSpec(memory_space=pltpu.VMEM)
    hbm = pl.BlockSpec(memory_space=pl.ANY)
    outs = (
        jax.ShapeDtypeStruct((3, groups, 128), F32),
        jax.ShapeDtypeStruct((3, 1, 6 * CAP), F32),
        jax.ShapeDtypeStruct(grid_mean, F32),
        jax.ShapeDtypeStruct((3, units), F32),
    )
    dma = pltpu.SemaphoreType.DMA

    def stay(x):
        return pltpu.with_memory_space_constraint(x, pltpu.HBM)

    kept, tail, cellv, force = pl.pallas_call(
        functools.partial(main_kernel, per, units),
        out_shape=outs,
        in_specs=[hbm] + [vmem] * 2 + [hbm] * 7,
        out_specs=(vmem,) * 4,
        scratch_shapes=[
            pltpu.VMEM((3, groups, 128), F32), pltpu.SMEM(grid_shift.shape, I32), pltpu.VMEM((3, units), F32),
            pltpu.VMEM(axis_index.shape, I32), pltpu.VMEM((groups, 128), I32), pltpu.VMEM((groups, 128), I32),
            pltpu.VMEM((1, contacts), I32), pltpu.VMEM((1, contacts), I32), pltpu.VMEM((1, contacts), F32),
            pltpu.VMEM((2,) + cells, I32), pltpu.VMEM((3,) + cells, F32), pltpu.VMEM(grid_mean, F32),
            pltpu.VMEM((2,) + cells, I32), pltpu.VMEM((8, 128), F32), pltpu.VMEM((per, PLANES + 1, 8, 128), F32),
            pltpu.VMEM((PLANES * HI, LO), F32), pltpu.VMEM((96, SLOT), F32), pltpu.VMEM((3, groups, 256), BF),
            pltpu.VMEM((6, 3, CAP), F32), pltpu.VMEM((6, 3, CAP), F32),
            pltpu.VMEM((6, 4, units), F32), pltpu.VMEM((6, 4, units), F32),
        ]
        + shift_scratch(axis_index.shape, I32) + shift_scratch(grid_mean, F32)
        + [dma((8,)), dma((64,)), dma((64,))],
        compiler_params=pltpu.CompilerParams(
            vmem_limit_bytes=48 * 2**20, collective_id=0, has_side_effects=True
        ),
        cost_estimate=pl.CostEstimate(flops=10**9, bytes_accessed=30_000_000, transcendentals=0),
    )(
        stay(grid_shift), velocities.reshape(3, groups, 128), particle_cells.reshape(2, groups, 128), stay(axis_index), stay(migrate_dir.reshape(groups, 128)),
        stay(migrate_slot.reshape(groups, 128)), stay(contact_particle.reshape(1, -1)),
        stay(contact_colloid.reshape(1, -1)), stay(contact_weight.reshape(1, -1)), stay(colloid_velocity),
    )
    return pl.pallas_call(
        last_kernel,
        out_shape=(
            jax.ShapeDtypeStruct(grid_mean, F32),
            jax.ShapeDtypeStruct((3, particles + 6 * CAP), F32),
            jax.ShapeDtypeStruct((3, units), F32),
        ),
        in_specs=[vmem] * 4,
        out_specs=(hbm,) * 3,
        scratch_shapes=[dma((8,))],
        compiler_params=pltpu.CompilerParams(vmem_limit_bytes=8 * 2**20),
    )(kept.reshape(3, 1, particles), tail, cellv, force)


def solution(mesh):
    flat = P(None, AXES)
    line = P(AXES)
    grid = P(None, *AXES)

    return jax.shard_map(
        body,
        mesh=mesh,
        in_specs=(flat, flat, P(), grid, line, line, line, line, line, flat),
        out_specs=(grid, flat, flat),
        check_vma=False,
    )
```

```python
import functools
import math

import jax
import jax.numpy as jnp
from jax import lax
from jax.experimental import pallas as pl
from jax.experimental.pallas import tpu as pltpu
from jax.sharding import PartitionSpec as P

CAP = 160
ANGLE = 130.0 * math.pi / 180.0
COS, SIN = math.cos(ANGLE), math.sin(ANGLE)
NT = (((1,), (1,)), ((), ()))
BF = jnp.bfloat16
F8 = jnp.float8_e4m3fn
F32 = jnp.float32
I32 = jnp.int32
HI, LO = 16, 256
PLANES = 10
PRE = 8.0
SLOT = 64
TOP = 1 << 19
EARLY = 1
AXES = ("gx", "gy", "gz")
MESH = pl.DeviceIdType.MESH
WAYS = [(x, y, z) for x in (-1, 0, 1) for y in (-1, 0, 1) for z in (-1, 0, 1) if (x, y, z) != (0, 0, 0)]


def split_index(c, low):
    if low & (low - 1) == 0:
        return c >> (low.bit_length() - 1), c & (low - 1)
    return c // low, c % low


def one():
    return jnp.ones((), BF)


def zero():
    return jnp.zeros((), BF)


def one_hot(row, count):
    kind = BF if count <= 256 else F32
    wide = lax.broadcasted_iota(I32, (count, row.shape[1]), 0).astype(F32).astype(kind)
    return jnp.where(wide == row.astype(F32).astype(kind), jnp.ones((), kind), jnp.zeros((), kind)).astype(BF)


def halves(x):
    high = x.astype(BF)
    return high, (x - high.astype(F32)).astype(BF)


def spread(rows, mask):
    return jnp.concatenate([mask * row for row in rows], axis=0)


def row_at(ref, plane, j, rows):
    return jnp.broadcast_to(ref[plane, j : j + 1], (rows, 128)).astype(BF)


def iotas(count):
    return [(lax.broadcasted_iota(I32, (16, 128), 0) + 16 * i).astype(F32).astype(BF) for i in range(count // 16)]


def pieces(x):
    x = x * PRE
    a = x.astype(F8).astype(F32)
    r = (x - a) * 16.0
    b = r.astype(F8).astype(F32)
    s = (r - b) * 16.0
    return a, b, s.astype(F8).astype(F32)


def stage_hist(st, cell, v):
    st[0] = ((cell & 127) | ((cell >> 11) << 7)).astype(F32)
    st[1] = ((cell >> 7) & 15).astype(F32)
    for k in range(3):
        for i, piece in enumerate(pieces(v[k])):
            st[2 + 3 * k + i] = piece


def hist_group(st, j, steps):
    low, high = row_at(st, 0, j, 16), row_at(st, 1, j, 16)
    hot = []
    for i in range(LO // 32):
        pair = [jnp.where(steps[2 * i + k] == low, one(), zero()) for k in range(2)]
        hot.append(jnp.concatenate(pair, axis=0).astype(F8))
    here = steps[0] == high
    rows = [jnp.where(here, row_at(st, 2 + q, j, 16), zero()) for q in range(PLANES - 1)]
    rows.append(jnp.where(here, one(), zero()))
    left = [jnp.concatenate(rows[2 * i : 2 * i + 2], axis=0).astype(F8) for i in range(PLANES // 2)]
    return jnp.concatenate(hot, axis=0), jnp.concatenate(left, axis=0)


def hist_add(acc, st, tiles, steps):
    groups = [hist_group(st.at[u], j, steps) for u in tiles for j in range(8)]
    left = jnp.concatenate([g[1] for g in groups], axis=1)
    hot = jnp.concatenate([g[0] for g in groups], axis=1)
    acc[...] += lax.dot_general(left, hot, NT, preferred_element_type=F32)


def mean_of(total, mean_ref):
    def plane(q):
        x = total[q * HI : (q + 1) * HI]
        return jnp.concatenate([x[:, :128], x[:, 128:]], axis=0)

    count = jnp.maximum(plane(9), 1.0)
    for k in range(3):
        sums = plane(3 * k) + plane(3 * k + 1) * (1.0 / 16) + plane(3 * k + 2) * (1.0 / 256)
        mean_ref[k] = sums * (1.0 / PRE) / count


def signs_of(index):
    return [jnp.where((index & (1 << i)) != 0, 1.0, -1.0) for i in range(3)]


def rotate(e, v):
    along = ((1.0 - COS) / 3.0) * (e[0] * v[0] + e[1] * v[1] + e[2] * v[2])
    turn = SIN / math.sqrt(3.0)
    out = []
    for i in range(3):
        j, k = (i + 1) % 3, (i + 2) % 3
        out.append(COS * v[i] + e[i] * along + turn * (e[j] * v[k] - e[k] * v[j]))
    return out


def make_table(mean_ref, axis_ref, table_ref, unit_ref):
    mean = [mean_ref[k] for k in range(3)]
    index = axis_ref[...]
    turned = rotate(signs_of(index), mean)
    offset = [mean[k] - turned[k] for k in range(3)]
    most = jnp.maximum(jnp.maximum(jnp.abs(offset[0]), jnp.abs(offset[1])), jnp.abs(offset[2]))
    most = jnp.max(jnp.max(most, axis=0, keepdims=True), axis=1, keepdims=True)
    most = jnp.maximum(most, 1e-25)
    scale = (TOP - 2.0) / most
    q = []
    for k in range(3):
        x = offset[k] * scale
        q.append((x + jnp.where(x >= 0.0, 0.5, -0.5)).astype(I32))
    last = q[2] + TOP
    table_ref[0] = (q[0] << 12) | (last >> 8)
    table_ref[1] = (q[1] << 12) | ((last & 255) << 4) | index
    unit_ref[...] = jnp.broadcast_to(most * (1.0 / (TOP - 2.0)), (8, 128))


def look_up(table_ref, cell):
    lane = cell & 127
    depth = table_ref.shape[1].bit_length() - 1
    bits = [(cell & (1 << (7 + b))) != 0 for b in range(depth)]

    def pick(word, b, at):
        if b < 0:
            row = jnp.broadcast_to(table_ref[word, at : at + 1], (8, 128))
            return jnp.take_along_axis(row, lane, axis=1, mode="promise_in_bounds")
        return jnp.where(bits[b], pick(word, b - 1, at + (1 << b)), pick(word, b - 1, at))

    return pick(0, depth - 1, 0), pick(1, depth - 1, 0)


def collide(table_ref, unit, cell, v):
    a, b = look_up(table_ref, cell)
    last = (((a & 4095) << 8) | ((b >> 4) & 255)) - TOP
    offset = [(x.astype(F32)) * unit for x in (a >> 12, b >> 12, last)]
    turned = rotate(signs_of(b), v)
    return [turned[k] + offset[k] for k in range(3)]


def beside(axis, sign):
    count = lax.axis_size(axis)
    return {axis: lax.rem(lax.axis_index(axis) + (sign + count), count)}


def kept_ways():
    return [w for w in WAYS if w[2] >= 0 or lax.axis_size("gz") > 2]


def greet():
    for way in kept_ways():
        pl.semaphore_signal(
            pltpu.get_barrier_semaphore(), inc=1, device_id=towards(way), device_id_type=MESH
        )


def towards(way):
    target = {}
    for axis, sign in zip(AXES, way):
        if sign:
            target.update(beside(axis, sign))
    return target


def send(src, dst, sems, number, axis, sign):
    copy = pltpu.make_async_remote_copy(
        src_ref=src, dst_ref=dst, send_sem=sems[0].at[number], recv_sem=sems[1].at[number],
        device_id=beside(axis, sign), device_id_type=MESH,
    )
    copy.start()
    return copy


def start_shift(x_ref, boxes, sems, first):
    zbox, xbox, ybox, faces = boxes
    n, cx, cy, _ = x_ref.shape
    for f in range(n):
        for i in range(cx):
            faces[0, f, i : i + 1, :] = x_ref[f, i, 0:1]
            faces[1, f, i : i + 1, :] = x_ref[f, i, cy - 1 : cy]
    copies = []
    for number, way in enumerate(kept_ways()):
        x, y, z = way
        if y:
            src, dst = faces.at[0 if y > 0 else 1], ybox.at[x + 1, 0 if y > 0 else 1, z + 1]
        elif x:
            src, dst = x_ref.at[:, 0 if x > 0 else cx - 1], xbox.at[0 if x > 0 else 1, z + 1]
        else:
            src, dst = x_ref, zbox.at[0 if z > 0 else 1]
        copy = pltpu.make_async_remote_copy(
            src_ref=src, dst_ref=dst, send_sem=sems[0].at[first + number], recv_sem=sems[1].at[first + number],
            device_id=towards((-x, -y, -z)), device_id_type=MESH,
        )
        copy.start()
        copies.append(copy)
    return copies


def finish_shift(copies, rows, flip, shift_ref, x_ref, boxes, put):
    zbox, xbox, ybox, _ = boxes
    n, cx, cy, nz = x_ref.shape
    deep = lax.axis_size("gz") > 2
    levels = (0, 1, 2) if deep else (2, 1, 2)
    for copy in copies:
        copy.wait()
    for f in range(n):
        up_x, up_y, up_z = (shift_ref[rows[f], dim] * flip > 0 for dim in range(3))

        def turn(parts):
            low, mid, high = parts
            end = mid.ndim - 1
            cut = lambda v, at, to: lax.slice_in_dim(v, at, to, axis=end)
            plus = jnp.concatenate([cut(mid, 1, nz), cut(high, 0, 1)], axis=end)
            minus = jnp.concatenate([cut(low, nz - 1, nz), cut(mid, 0, nz - 1)], axis=end)
            return jnp.where(up_z, plus, minus)

        def edge(z):
            pick = [
                jnp.where(up_x, ybox[2, s, z, f, 0:1], ybox[0, s, z, f, cx - 1 : cx]) for s in range(2)
            ]
            return jnp.where(up_y, pick[0], pick[1])

        core = turn([zbox[1 if deep else 0, f], x_ref[f], zbox[0, f]])
        side = turn([jnp.where(up_x, xbox[0, z, f], xbox[1, z, f]) for z in levels])
        face = turn([jnp.where(up_y, ybox[1, 0, z, f], ybox[1, 1, z, f]) for z in levels])
        corner = turn([edge(z) for z in levels])
        for i in range(cx):
            plus = core[i + 1] if i + 1 < cx else side
            minus = core[i - 1] if i > 0 else side
            x = jnp.where(up_x, plus, minus)
            plus = face[i + 1 : i + 2] if i + 1 < cx else corner
            minus = face[i - 1 : i] if i > 0 else corner
            row = jnp.where(up_x, plus, minus)
            plus = jnp.concatenate([x[1:], row], axis=0)
            minus = jnp.concatenate([row, x[: cy - 1]], axis=0)
            put(f, i, jnp.where(up_y, plus, minus))


def shift_scratch(shape, kind):
    n, cx, cy, nz = shape
    return [
        pltpu.VMEM((2, n, cx, cy, nz), kind), pltpu.VMEM((2, 3, n, cy, nz), kind),
        pltpu.VMEM((3, 2, 3, n, cx, nz), kind), pltpu.VMEM((2, n, cx, nz), kind),
    ]


def contact_places(colloid, units):
    size_x, size_y, size_z = (lax.axis_size(a) for a in AXES)
    mine_x, mine_y, mine_z = (lax.axis_index(a) for a in AXES)
    owner, member = split_index(colloid, units)
    rest, own_z = split_index(owner, size_z)
    own_x, own_y = split_index(rest, size_y)

    def apart(own, mine, size):
        return split_index(own - mine + size, size)[1]

    apart_x, apart_y, apart_z = apart(own_x, mine_x, size_x), apart(own_y, mine_y, size_y), apart(own_z, mine_z, size_z)
    code = jnp.full(colloid.shape, 6, I32)
    pairs = (
        (apart_x, 1), (apart_x, size_x - 1), (apart_y, 1),
        (apart_y, size_y - 1), (apart_z, 1), (apart_z, size_z - 1),
    )
    for number, (gap, to) in reversed(list(enumerate(pairs))):
        code = jnp.where(gap == to, number, code)
    return code, member


def main_kernel(
    per, units, shift_hbm, v_in, cs, axis_hbm, dir_hbm, slot_hbm, who_hbm, colloid_hbm, weight_hbm, drift_hbm,
    kept_ref, tail_ref, cellv_ref, force_ref,
    vs, shift_ref, drift_ref, field, dirs, slots, who, colloid, weight, axes, mean, field_mean, table, unit_ref, st, acc, moved, book,
    going, coming, pushes, pulls, *rest
):
    boxes_a, boxes_b, (local_sem, out_sem, in_sem) = rest[:4], rest[4:8], rest[8:]
    sems = (out_sem, in_sem)
    cx, cy, nz = axis_hbm.shape[1:]
    groups = v_in.shape[1]
    loops0, loops = groups // (8 * per[0]), groups // (8 * per[1])

    def fetch(src, dst, number):
        copy = pltpu.make_async_copy(src, dst, local_sem.at[number])
        copy.start()
        return copy

    first = [fetch(axis_hbm, field, 0), fetch(shift_hbm, shift_ref, 7)]
    late = [fetch(dir_hbm, dirs, 1), fetch(slot_hbm, slots, 2), fetch(who_hbm, who, 3)]
    late += [fetch(colloid_hbm, colloid, 4), fetch(weight_hbm, weight, 5), fetch(drift_hbm, drift_ref, 6)]
    greet()

    steps = iotas(LO)

    def rows_of(t, u, many):
        return pl.ds(pl.multiple_of((t * many + u) * 8, 8), 8)

    def put_axis(f, i, value):
        axes[f, i * cy : (i + 1) * cy, :] = value

    acc[...] = jnp.zeros_like(acc)

    def step0(t, carry):
        for u in range(per[0]):
            at = rows_of(t, u, per[0])
            stage_hist(st.at[u], cs[0, at], [v_in[k, at] for k in range(3)])
        hist_add(acc, st, range(per[0]), steps)
        return carry

    lax.fori_loop(0, EARLY, step0, 0)
    pl.semaphore_wait(pltpu.get_barrier_semaphore(), len(kept_ways()))
    for copy in first:
        copy.wait()
    copies = start_shift(field, boxes_a, sems, 0)
    lax.fori_loop(EARLY, loops0, step0, 0)
    finish_shift(copies, (0, 1), 1, shift_ref, field, boxes_a, put_axis)
    mean_of(acc[...], mean)
    for copy in late:
        copy.wait()
    make_table(mean, axes.at[0], table, unit_ref)
    acc[...] = jnp.zeros_like(acc)

    def step1(t, carry):
        unit = unit_ref[...]
        for u in range(per[1]):
            at = rows_of(t, u, per[1])
            new = collide(table, unit, cs[0, at], [v_in[k, at] for k in range(3)])
            for k in range(3):
                vs[k, at] = new[k]
            stage_hist(st.at[u], cs[1, at], new)
        hist_add(acc, st, range(per[1]), steps)
        return carry

    lax.fori_loop(0, loops, step1, 0)
    mean_of(acc[...], mean)
    make_table(mean, axes.at[1], table, unit_ref)
    for k in range(3):
        for i in range(cx):
            field_mean[k, i] = mean[k, i * cy : (i + 1) * cy]
    moved[...] = jnp.zeros_like(moved)
    narrow = iotas(SLOT)

    def leave_group(ref, j):
        low, high = row_at(ref, 0, j, 16), row_at(ref, 1, j, 16)
        hot = jnp.concatenate([jnp.where(wide == low, one(), zero()) for wide in narrow], axis=0)
        here = narrow[0] == high
        rows = [jnp.where(here, row_at(ref, 2 + q, j, 16), zero()) for q in range(6)]
        return hot, jnp.concatenate(rows, axis=0)

    def step2(t, carry):
        unit = unit_ref[...]
        hots, lefts = [], []
        for u in range(per[1]):
            at = rows_of(t, u, per[1])
            new = collide(table, unit, cs[1, at], [vs[k, at] for k in range(3)])
            code = dirs[at]
            stays = code == 0
            goal = jnp.where(stays, -SLOT, (code - 1) * CAP + slots[at])
            st[u, 0] = (goal & (SLOT - 1)).astype(F32)
            st[u, 1] = (goal >> (SLOT.bit_length() - 1)).astype(F32)
            for k in range(3):
                kept_ref[k, at] = jnp.where(stays, new[k], 0.0)
                high, low = halves(new[k])
                st[u, 2 + 2 * k] = high.astype(F32)
                st[u, 3 + 2 * k] = low.astype(F32)
        for u in range(0, per[1], 2):
            at = pl.ds(pl.multiple_of((t * per[1] + u) * 8, 16), 16)
            for k in range(3):
                for i in range(2):
                    both_tiles = jnp.concatenate([st[u, 2 + 2 * k + i], st[u + 1, 2 + 2 * k + i]], axis=0)
                    book[k, at, i * 128 : (i + 1) * 128] = both_tiles.astype(BF)
        for u in range(per[1]):
            for j in range(8):
                hot, left = leave_group(st.at[u], j)
                hots.append(hot)
                lefts.append(left)
        moved[...] += lax.dot_general(
            jnp.concatenate(lefts, axis=1), jnp.concatenate(hots, axis=1), NT, preferred_element_type=F32
        )
        return carry

    def put_mean(f, i, value):
        cellv_ref[f, i] = value

    rows_of_shift = [shift_ref.shape[0] - 1] * 3
    means = start_shift(field_mean, boxes_b, sems, 26)
    lax.fori_loop(0, loops, step2, 0)

    for k in range(3):
        value = moved[32 * k : 32 * k + 16] + moved[32 * k + 16 : 32 * k + 32]
        for d in range(6):
            at, end, parts = d * CAP, (d + 1) * CAP, []
            while at < end:
                r, c = at // SLOT, at % SLOT
                size = min(SLOT - c, end - at)
                parts.append(value[r : r + 1, c : c + size])
                at += size
            going[d, k : k + 1, :] = jnp.concatenate(parts, axis=1)
    copies = [
        send(going.at[d], coming.at[d], sems, 52 + d, AXES[d // 2], 1 - 2 * (d % 2)) for d in range(6)
    ]

    contacts = who.shape[1]
    chunk = min(512, contacts)
    sums = jnp.zeros((8 * 16, units), F32)
    pages = book[...].reshape(3 * groups, 256)
    for c in range(contacts // chunk):
        at = slice(c * chunk, (c + 1) * chunk)
        hi, lo = split_index(who[0:1, at], 128)
        hot = one_hot(lo, 128)
        got = jnp.dot(pages, jnp.concatenate([hot, hot], axis=0), preferred_element_type=F32)
        here = lax.broadcasted_iota(I32, (groups, chunk), 0) == hi
        force = weight[0:1, at]
        rows = []
        for k in range(3):
            mine = jnp.where(here, got[k * groups : (k + 1) * groups], 0.0)
            rows.extend(halves(force * jnp.sum(mine, axis=0, keepdims=True)))
        rows.extend(halves(force))
        code, member = contact_places(colloid[0:1, at], units)
        sums = sums + lax.dot_general(
            spread(rows, one_hot(code, 16)), one_hot(member, units), NT, preferred_element_type=F32
        )
    totals = [sums[32 * k : 32 * k + 16] + sums[32 * k + 16 : 32 * k + 32] for k in range(4)]
    total = jnp.concatenate([x[6:7] for x in totals], axis=0)
    for d in range(6):
        for k in range(4):
            pushes[d, k : k + 1, :] = totals[k][d : d + 1]
    more = [
        send(pushes.at[d], pulls.at[d], sems, 58 + d, AXES[d // 2], 1 - 2 * (d % 2)) for d in range(6)
    ]
    finish_shift(means, rows_of_shift, -1, shift_ref, field_mean, boxes_b, put_mean)
    for d, copy in enumerate(copies):
        copy.wait()
        for k in range(3):
            tail_ref[k, :, d * CAP : (d + 1) * CAP] = coming[d, k : k + 1]
    for d, copy in enumerate(more):
        copy.wait()
        total = total + pulls[d]
    sum_w = total[3:4]
    force_ref[...] = (total[0:3] - sum_w * drift_ref[...]) / jnp.maximum(sum_w, 1.0)


def last_kernel(kept_ref, tail_ref, cellv_ref, force_ref, cellv_hbm, out_hbm, force_hbm, sem):
    particles, extra = kept_ref.shape[2], tail_ref.shape[2]
    copies = []
    for k in range(3):
        row = pl.ds(k, 1)
        copies.append((kept_ref.at[k], out_hbm.at[row, pl.ds(0, particles)]))
        copies.append((tail_ref.at[k], out_hbm.at[row, pl.ds(particles, extra)]))
    copies += [(cellv_ref, cellv_hbm), (force_ref, force_hbm)]
    copies = [pltpu.make_async_copy(src, dst, sem.at[i]) for i, (src, dst) in enumerate(copies)]
    for copy in copies:
        copy.start()
    for copy in copies:
        copy.wait()


def body(
    velocities, particle_cells, grid_shift, axis_index, migrate_dir, migrate_slot,
    contact_colloid, contact_particle, contact_weight, colloid_velocity,
):
    _, cx, cy, nlo = axis_index.shape
    particles = velocities.shape[1]
    units = colloid_velocity.shape[1]
    contacts = contact_weight.shape[0]
    groups = particles // 128
    cells = (cx * cy, nlo)
    if cells != (2 * HI, 128) or particles % 4096 or 6 * CAP > 16 * SLOT:
        raise ValueError("sizes")
    per = [next(p for p in sizes if groups % (8 * p) == 0) for sizes in ((8, 4), (20, 8, 4))]
    grid_mean = (3, cx, cy, nlo)
    vmem = pl.BlockSpec(memory_space=pltpu.VMEM)
    hbm = pl.BlockSpec(memory_space=pl.ANY)
    outs = (
        jax.ShapeDtypeStruct((3, groups, 128), F32),
        jax.ShapeDtypeStruct((3, 1, 6 * CAP), F32),
        jax.ShapeDtypeStruct(grid_mean, F32),
        jax.ShapeDtypeStruct((3, units), F32),
    )
    dma = pltpu.SemaphoreType.DMA

    def stay(x):
        return pltpu.with_memory_space_constraint(x, pltpu.HBM)

    kept, tail, cellv, force = pl.pallas_call(
        functools.partial(main_kernel, per, units),
        out_shape=outs,
        in_specs=[hbm] + [vmem] * 2 + [hbm] * 7,
        out_specs=(vmem,) * 4,
        scratch_shapes=[
            pltpu.VMEM((3, groups, 128), F32), pltpu.SMEM(grid_shift.shape, I32), pltpu.VMEM((3, units), F32),
            pltpu.VMEM(axis_index.shape, I32), pltpu.VMEM((groups, 128), I32), pltpu.VMEM((groups, 128), I32),
            pltpu.VMEM((1, contacts), I32), pltpu.VMEM((1, contacts), I32), pltpu.VMEM((1, contacts), F32),
            pltpu.VMEM((2,) + cells, I32), pltpu.VMEM((3,) + cells, F32), pltpu.VMEM(grid_mean, F32),
            pltpu.VMEM((2,) + cells, I32), pltpu.VMEM((8, 128), F32), pltpu.VMEM((max(per), PLANES + 1, 8, 128), F32),
            pltpu.VMEM((PLANES * HI, LO), F32), pltpu.VMEM((96, SLOT), F32), pltpu.VMEM((3, groups, 256), BF),
            pltpu.VMEM((6, 3, CAP), F32), pltpu.VMEM((6, 3, CAP), F32),
            pltpu.VMEM((6, 4, units), F32), pltpu.VMEM((6, 4, units), F32),
        ]
        + shift_scratch(axis_index.shape, I32) + shift_scratch(grid_mean, F32)
        + [dma((8,)), dma((64,)), dma((64,))],
        compiler_params=pltpu.CompilerParams(
            vmem_limit_bytes=48 * 2**20, collective_id=0, has_side_effects=True
        ),
        cost_estimate=pl.CostEstimate(flops=10**9, bytes_accessed=30_000_000, transcendentals=0),
    )(
        stay(grid_shift), velocities.reshape(3, groups, 128), particle_cells.reshape(2, groups, 128), stay(axis_index), stay(migrate_dir.reshape(groups, 128)),
        stay(migrate_slot.reshape(groups, 128)), stay(contact_particle.reshape(1, -1)),
        stay(contact_colloid.reshape(1, -1)), stay(contact_weight.reshape(1, -1)), stay(colloid_velocity),
    )
    return pl.pallas_call(
        last_kernel,
        out_shape=(
            jax.ShapeDtypeStruct(grid_mean, F32),
            jax.ShapeDtypeStruct((3, particles + 6 * CAP), F32),
            jax.ShapeDtypeStruct((3, units), F32),
        ),
        in_specs=[vmem] * 4,
        out_specs=(hbm,) * 3,
        scratch_shapes=[dma((8,))],
        compiler_params=pltpu.CompilerParams(vmem_limit_bytes=8 * 2**20),
    )(kept.reshape(3, 1, particles), tail, cellv, force)


def solution(mesh):
    flat = P(None, AXES)
    line = P(AXES)
    grid = P(None, *AXES)

    return jax.shard_map(
        body,
        mesh=mesh,
        in_specs=(flat, flat, P(), grid, line, line, line, line, line, flat),
        out_specs=(grid, flat, flat),
        check_vma=False,
    )
```

```python
import functools
import math

import jax
import jax.numpy as jnp
from jax import lax
from jax.experimental import pallas as pl
from jax.experimental.pallas import tpu as pltpu
from jax.sharding import PartitionSpec as P

CAP = 160
ANGLE = 130.0 * math.pi / 180.0
COS, SIN = math.cos(ANGLE), math.sin(ANGLE)
NT = (((1,), (1,)), ((), ()))
BF = jnp.bfloat16
F8 = jnp.float8_e4m3fn
F32 = jnp.float32
I32 = jnp.int32
HI, LO = 16, 256
PLANES = 10
PRE = 8.0
SLOT = 64
TOP = 1 << 19
EARLY = 1
AXES = ("gx", "gy", "gz")
MESH = pl.DeviceIdType.MESH
WAYS = [(x, y, z) for x in (-1, 0, 1) for y in (-1, 0, 1) for z in (-1, 0, 1) if (x, y, z) != (0, 0, 0)]
WAYS.sort(key=lambda way: (way[0] == 0, -sum(map(abs, way))))


def split_index(c, low):
    if low & (low - 1) == 0:
        return c >> (low.bit_length() - 1), c & (low - 1)
    return c // low, c % low


def one():
    return jnp.ones((), BF)


def zero():
    return jnp.zeros((), BF)


def one_hot(row, count):
    kind = BF if count <= 256 else F32
    wide = lax.broadcasted_iota(I32, (count, row.shape[1]), 0).astype(F32).astype(kind)
    return jnp.where(wide == row.astype(F32).astype(kind), jnp.ones((), kind), jnp.zeros((), kind)).astype(BF)


def halves(x):
    high = x.astype(BF)
    return high, (x - high.astype(F32)).astype(BF)


def spread(rows, mask):
    return jnp.concatenate([mask * row for row in rows], axis=0)


def row_at(ref, plane, j, rows):
    return jnp.broadcast_to(ref[plane, j : j + 1], (rows, 128)).astype(BF)


def iotas(count):
    return [(lax.broadcasted_iota(I32, (16, 128), 0) + 16 * i).astype(F32).astype(BF) for i in range(count // 16)]


def pieces(x):
    x = x * PRE
    a = x.astype(F8).astype(F32)
    r = (x - a) * 16.0
    b = r.astype(F8).astype(F32)
    s = (r - b) * 16.0
    return a, b, s.astype(F8).astype(F32)


def stage_hist(st, cell, v):
    st[0] = ((cell & 127) | ((cell >> 11) << 7)).astype(F32)
    st[1] = ((cell >> 7) & 15).astype(F32)
    for k in range(3):
        for i, piece in enumerate(pieces(v[k])):
            st[2 + 3 * k + i] = piece


def hist_group(st, j, steps):
    low, high = row_at(st, 0, j, 16), row_at(st, 1, j, 16)
    hot = []
    for i in range(LO // 32):
        pair = [jnp.where(steps[2 * i + k] == low, one(), zero()) for k in range(2)]
        hot.append(jnp.concatenate(pair, axis=0).astype(F8))
    here = steps[0] == high
    rows = [jnp.where(here, row_at(st, 2 + q, j, 16), zero()) for q in range(PLANES - 1)]
    rows.append(jnp.where(here, one(), zero()))
    left = [jnp.concatenate(rows[2 * i : 2 * i + 2], axis=0).astype(F8) for i in range(PLANES // 2)]
    return jnp.concatenate(hot, axis=0), jnp.concatenate(left, axis=0)


def hist_add(acc, st, tiles, steps):
    groups = [hist_group(st.at[u], j, steps) for u in tiles for j in range(8)]
    left = jnp.concatenate([g[1] for g in groups], axis=1)
    hot = jnp.concatenate([g[0] for g in groups], axis=1)
    acc[...] += lax.dot_general(left, hot, NT, preferred_element_type=F32)


def mean_of(total, mean_ref):
    def plane(q):
        x = total[q * HI : (q + 1) * HI]
        return jnp.concatenate([x[:, :128], x[:, 128:]], axis=0)

    count = jnp.maximum(plane(9), 1.0)
    for k in range(3):
        sums = plane(3 * k) + plane(3 * k + 1) * (1.0 / 16) + plane(3 * k + 2) * (1.0 / 256)
        mean_ref[k] = sums * (1.0 / PRE) / count


def signs_of(index):
    return [jnp.where((index & (1 << i)) != 0, 1.0, -1.0) for i in range(3)]


def rotate(e, v):
    along = ((1.0 - COS) / 3.0) * (e[0] * v[0] + e[1] * v[1] + e[2] * v[2])
    turn = SIN / math.sqrt(3.0)
    out = []
    for i in range(3):
        j, k = (i + 1) % 3, (i + 2) % 3
        out.append(COS * v[i] + e[i] * along + turn * (e[j] * v[k] - e[k] * v[j]))
    return out


def make_table(mean_ref, axis_ref, table_ref, unit_ref):
    mean = [mean_ref[k] for k in range(3)]
    index = axis_ref[...]
    turned = rotate(signs_of(index), mean)
    offset = [mean[k] - turned[k] for k in range(3)]
    most = jnp.maximum(jnp.maximum(jnp.abs(offset[0]), jnp.abs(offset[1])), jnp.abs(offset[2]))
    most = jnp.max(jnp.max(most, axis=0, keepdims=True), axis=1, keepdims=True)
    most = jnp.maximum(most, 1e-25)
    scale = (TOP - 2.0) / most
    q = []
    for k in range(3):
        x = offset[k] * scale
        q.append((x + jnp.where(x >= 0.0, 0.5, -0.5)).astype(I32))
    last = q[2] + TOP
    table_ref[0] = (q[0] << 12) | (last >> 8)
    table_ref[1] = (q[1] << 12) | ((last & 255) << 4) | index
    unit_ref[...] = jnp.broadcast_to(most * (1.0 / (TOP - 2.0)), (8, 128))


def look_up(table_ref, cell):
    lane = cell & 127
    depth = table_ref.shape[1].bit_length() - 1
    bits = [(cell & (1 << (7 + b))) != 0 for b in range(depth)]

    def pick(word, b, at):
        if b < 0:
            row = jnp.broadcast_to(table_ref[word, at : at + 1], (8, 128))
            return jnp.take_along_axis(row, lane, axis=1, mode="promise_in_bounds")
        return jnp.where(bits[b], pick(word, b - 1, at + (1 << b)), pick(word, b - 1, at))

    return pick(0, depth - 1, 0), pick(1, depth - 1, 0)


def collide(table_ref, unit, cell, v):
    a, b = look_up(table_ref, cell)
    last = (((a & 4095) << 8) | ((b >> 4) & 255)) - TOP
    offset = [(x.astype(F32)) * unit for x in (a >> 12, b >> 12, last)]
    turned = rotate(signs_of(b), v)
    return [turned[k] + offset[k] for k in range(3)]


def beside(axis, sign):
    count = lax.axis_size(axis)
    return {axis: lax.rem(lax.axis_index(axis) + (sign + count), count)}


def kept_ways():
    return [w for w in WAYS if w[2] >= 0 or lax.axis_size("gz") > 2]


def greet():
    for way in kept_ways():
        pl.semaphore_signal(
            pltpu.get_barrier_semaphore(), inc=1, device_id=towards(way), device_id_type=MESH
        )


def towards(way):
    target = {}
    for axis, sign in zip(AXES, way):
        if sign:
            target.update(beside(axis, sign))
    return target


def send(src, dst, sems, number, axis, sign):
    copy = pltpu.make_async_remote_copy(
        src_ref=src, dst_ref=dst, send_sem=sems[0].at[number], recv_sem=sems[1].at[number],
        device_id=beside(axis, sign), device_id_type=MESH,
    )
    copy.start()
    return copy


def start_shift(x_ref, boxes, sems, first):
    zbox, xbox, ybox, faces = boxes
    n, cx, cy, _ = x_ref.shape
    for f in range(n):
        for i in range(cx):
            faces[0, f, i : i + 1, :] = x_ref[f, i, 0:1]
            faces[1, f, i : i + 1, :] = x_ref[f, i, cy - 1 : cy]
    copies = []
    for number, way in enumerate(kept_ways()):
        x, y, z = way
        if y:
            src, dst = faces.at[0 if y > 0 else 1], ybox.at[x + 1, 0 if y > 0 else 1, z + 1]
        elif x:
            src, dst = x_ref.at[:, 0 if x > 0 else cx - 1], xbox.at[0 if x > 0 else 1, z + 1]
        else:
            src, dst = x_ref, zbox.at[0 if z > 0 else 1]
        copy = pltpu.make_async_remote_copy(
            src_ref=src, dst_ref=dst, send_sem=sems[0].at[first + number], recv_sem=sems[1].at[first + number],
            device_id=towards((-x, -y, -z)), device_id_type=MESH,
        )
        copy.start()
        copies.append(copy)
    return copies


def finish_shift(copies, rows, flip, shift_ref, x_ref, boxes, put):
    zbox, xbox, ybox, _ = boxes
    n, cx, cy, nz = x_ref.shape
    deep = lax.axis_size("gz") > 2
    levels = (0, 1, 2) if deep else (2, 1, 2)
    for copy in copies:
        copy.wait()
    for f in range(n):
        up_x, up_y, up_z = (shift_ref[rows[f], dim] * flip > 0 for dim in range(3))

        def turn(parts):
            low, mid, high = parts
            end = mid.ndim - 1
            cut = lambda v, at, to: lax.slice_in_dim(v, at, to, axis=end)
            plus = jnp.concatenate([cut(mid, 1, nz), cut(high, 0, 1)], axis=end)
            minus = jnp.concatenate([cut(low, nz - 1, nz), cut(mid, 0, nz - 1)], axis=end)
            return jnp.where(up_z, plus, minus)

        def edge(z):
            pick = [
                jnp.where(up_x, ybox[2, s, z, f, 0:1], ybox[0, s, z, f, cx - 1 : cx]) for s in range(2)
            ]
            return jnp.where(up_y, pick[0], pick[1])

        core = turn([zbox[1 if deep else 0, f], x_ref[f], zbox[0, f]])
        side = turn([jnp.where(up_x, xbox[0, z, f], xbox[1, z, f]) for z in levels])
        face = turn([jnp.where(up_y, ybox[1, 0, z, f], ybox[1, 1, z, f]) for z in levels])
        corner = turn([edge(z) for z in levels])
        for i in range(cx):
            plus = core[i + 1] if i + 1 < cx else side
            minus = core[i - 1] if i > 0 else side
            x = jnp.where(up_x, plus, minus)
            plus = face[i + 1 : i + 2] if i + 1 < cx else corner
            minus = face[i - 1 : i] if i > 0 else corner
            row = jnp.where(up_x, plus, minus)
            plus = jnp.concatenate([x[1:], row], axis=0)
            minus = jnp.concatenate([row, x[: cy - 1]], axis=0)
            put(f, i, jnp.where(up_y, plus, minus))


def shift_scratch(shape, kind):
    n, cx, cy, nz = shape
    return [
        pltpu.VMEM((2, n, cx, cy, nz), kind), pltpu.VMEM((2, 3, n, cy, nz), kind),
        pltpu.VMEM((3, 2, 3, n, cx, nz), kind), pltpu.VMEM((2, n, cx, nz), kind),
    ]


def contact_places(colloid, units):
    size_x, size_y, size_z = (lax.axis_size(a) for a in AXES)
    mine_x, mine_y, mine_z = (lax.axis_index(a) for a in AXES)
    owner, member = split_index(colloid, units)
    rest, own_z = split_index(owner, size_z)
    own_x, own_y = split_index(rest, size_y)

    def apart(own, mine, size):
        return split_index(own - mine + size, size)[1]

    apart_x, apart_y, apart_z = apart(own_x, mine_x, size_x), apart(own_y, mine_y, size_y), apart(own_z, mine_z, size_z)
    code = jnp.full(colloid.shape, 6, I32)
    pairs = (
        (apart_x, 1), (apart_x, size_x - 1), (apart_y, 1),
        (apart_y, size_y - 1), (apart_z, 1), (apart_z, size_z - 1),
    )
    for number, (gap, to) in reversed(list(enumerate(pairs))):
        code = jnp.where(gap == to, number, code)
    return code, member


def main_kernel(
    per, units, shift_hbm, v_in, cs, axis_hbm, dir_hbm, slot_hbm, who_hbm, colloid_hbm, weight_hbm, drift_hbm,
    kept_ref, tail_ref, cellv_ref, force_ref,
    vs, shift_ref, drift_ref, field, dirs, slots, who, colloid, weight, axes, mean, field_mean, table, unit_ref, st, acc, moved, book,
    going, coming, pushes, pulls, *rest
):
    boxes_a, boxes_b, (local_sem, out_sem, in_sem) = rest[:4], rest[4:8], rest[8:]
    sems = (out_sem, in_sem)
    cx, cy, nz = axis_hbm.shape[1:]
    groups = v_in.shape[1]
    loops0, loops = groups // (8 * per[0]), groups // (8 * per[1])

    def fetch(src, dst, number):
        copy = pltpu.make_async_copy(src, dst, local_sem.at[number])
        copy.start()
        return copy

    first = [fetch(axis_hbm, field, 0), fetch(shift_hbm, shift_ref, 7)]
    late = [fetch(dir_hbm, dirs, 1), fetch(slot_hbm, slots, 2), fetch(who_hbm, who, 3)]
    late += [fetch(colloid_hbm, colloid, 4), fetch(weight_hbm, weight, 5), fetch(drift_hbm, drift_ref, 6)]
    greet()

    steps = iotas(LO)

    def rows_of(t, u, many):
        return pl.ds(pl.multiple_of((t * many + u) * 8, 8), 8)

    def put_axis(f, i, value):
        axes[f, i * cy : (i + 1) * cy, :] = value

    acc[...] = jnp.zeros_like(acc)

    def step0(t, carry):
        for u in range(per[0]):
            at = rows_of(t, u, per[0])
            stage_hist(st.at[u], cs[0, at], [v_in[k, at] for k in range(3)])
        hist_add(acc, st, range(per[0]), steps)
        return carry

    lax.fori_loop(0, EARLY, step0, 0)
    pl.semaphore_wait(pltpu.get_barrier_semaphore(), len(kept_ways()))
    for copy in first:
        copy.wait()
    copies = start_shift(field, boxes_a, sems, 0)
    lax.fori_loop(EARLY, loops0, step0, 0)
    finish_shift(copies, (0, 1), 1, shift_ref, field, boxes_a, put_axis)
    mean_of(acc[...], mean)
    for copy in late:
        copy.wait()
    make_table(mean, axes.at[0], table, unit_ref)
    acc[...] = jnp.zeros_like(acc)

    def step1(t, carry):
        unit = unit_ref[...]
        for u in range(per[1]):
            at = rows_of(t, u, per[1])
            new = collide(table, unit, cs[0, at], [v_in[k, at] for k in range(3)])
            for k in range(3):
                vs[k, at] = new[k]
            stage_hist(st.at[u], cs[1, at], new)
        hist_add(acc, st, range(per[1]), steps)
        return carry

    lax.fori_loop(0, loops, step1, 0)
    mean_of(acc[...], mean)
    make_table(mean, axes.at[1], table, unit_ref)
    for k in range(3):
        for i in range(cx):
            field_mean[k, i] = mean[k, i * cy : (i + 1) * cy]
    moved[...] = jnp.zeros_like(moved)
    narrow = iotas(SLOT)

    def leave_group(ref, j):
        low, high = row_at(ref, 0, j, 16), row_at(ref, 1, j, 16)
        hot = jnp.concatenate([jnp.where(wide == low, one(), zero()) for wide in narrow], axis=0)
        here = narrow[0] == high
        rows = [jnp.where(here, row_at(ref, 2 + q, j, 16), zero()) for q in range(6)]
        return hot, jnp.concatenate(rows, axis=0)

    def step2(t, carry):
        unit = unit_ref[...]
        hots, lefts = [], []
        for u in range(per[1]):
            at = rows_of(t, u, per[1])
            new = collide(table, unit, cs[1, at], [vs[k, at] for k in range(3)])
            code = dirs[at]
            stays = code == 0
            goal = jnp.where(stays, -SLOT, (code - 1) * CAP + slots[at])
            st[u, 0] = (goal & (SLOT - 1)).astype(F32)
            st[u, 1] = (goal >> (SLOT.bit_length() - 1)).astype(F32)
            for k in range(3):
                kept_ref[k, at] = jnp.where(stays, new[k], 0.0)
                high, low = halves(new[k])
                st[u, 2 + 2 * k] = high.astype(F32)
                st[u, 3 + 2 * k] = low.astype(F32)
        for u in range(0, per[1], 2):
            at = pl.ds(pl.multiple_of((t * per[1] + u) * 8, 16), 16)
            for k in range(3):
                for i in range(2):
                    both_tiles = jnp.concatenate([st[u, 2 + 2 * k + i], st[u + 1, 2 + 2 * k + i]], axis=0)
                    book[k, at, i * 128 : (i + 1) * 128] = both_tiles.astype(BF)
        for u in range(per[1]):
            for j in range(8):
                hot, left = leave_group(st.at[u], j)
                hots.append(hot)
                lefts.append(left)
        moved[...] += lax.dot_general(
            jnp.concatenate(lefts, axis=1), jnp.concatenate(hots, axis=1), NT, preferred_element_type=F32
        )
        return carry

    def put_mean(f, i, value):
        cellv_ref[f, i] = value

    rows_of_shift = [shift_ref.shape[0] - 1] * 3
    means = start_shift(field_mean, boxes_b, sems, 26)
    lax.fori_loop(0, loops, step2, 0)

    for k in range(3):
        value = moved[32 * k : 32 * k + 16] + moved[32 * k + 16 : 32 * k + 32]
        for d in range(6):
            at, end, parts = d * CAP, (d + 1) * CAP, []
            while at < end:
                r, c = at // SLOT, at % SLOT
                size = min(SLOT - c, end - at)
                parts.append(value[r : r + 1, c : c + size])
                at += size
            going[d, k : k + 1, :] = jnp.concatenate(parts, axis=1)
    copies = [
        send(going.at[d], coming.at[d], sems, 52 + d, AXES[d // 2], 1 - 2 * (d % 2)) for d in range(6)
    ]

    contacts = who.shape[1]
    chunk = min(512, contacts)
    sums = jnp.zeros((8 * 16, units), F32)
    pages = book[...].reshape(3 * groups, 256)
    for c in range(contacts // chunk):
        at = slice(c * chunk, (c + 1) * chunk)
        hi, lo = split_index(who[0:1, at], 128)
        hot = one_hot(lo, 128)
        got = jnp.dot(pages, jnp.concatenate([hot, hot], axis=0), preferred_element_type=F32)
        here = lax.broadcasted_iota(I32, (groups, chunk), 0) == hi
        force = weight[0:1, at]
        rows = []
        for k in range(3):
            mine = jnp.where(here, got[k * groups : (k + 1) * groups], 0.0)
            rows.extend(halves(force * jnp.sum(mine, axis=0, keepdims=True)))
        rows.extend(halves(force))
        code, member = contact_places(colloid[0:1, at], units)
        sums = sums + lax.dot_general(
            spread(rows, one_hot(code, 16)), one_hot(member, units), NT, preferred_element_type=F32
        )
    totals = [sums[32 * k : 32 * k + 16] + sums[32 * k + 16 : 32 * k + 32] for k in range(4)]
    total = jnp.concatenate([x[6:7] for x in totals], axis=0)
    for d in range(6):
        for k in range(4):
            pushes[d, k : k + 1, :] = totals[k][d : d + 1]
    more = [
        send(pushes.at[d], pulls.at[d], sems, 58 + d, AXES[d // 2], 1 - 2 * (d % 2)) for d in range(6)
    ]
    finish_shift(means, rows_of_shift, -1, shift_ref, field_mean, boxes_b, put_mean)
    for d, copy in enumerate(copies):
        copy.wait()
        for k in range(3):
            tail_ref[k, :, d * CAP : (d + 1) * CAP] = coming[d, k : k + 1]
    for d, copy in enumerate(more):
        copy.wait()
        total = total + pulls[d]
    sum_w = total[3:4]
    force_ref[...] = (total[0:3] - sum_w * drift_ref[...]) / jnp.maximum(sum_w, 1.0)


def last_kernel(kept_ref, tail_ref, cellv_ref, force_ref, cellv_hbm, out_hbm, force_hbm, sem):
    particles, extra = kept_ref.shape[2], tail_ref.shape[2]
    copies = []
    for k in range(3):
        row = pl.ds(k, 1)
        copies.append((kept_ref.at[k], out_hbm.at[row, pl.ds(0, particles)]))
        copies.append((tail_ref.at[k], out_hbm.at[row, pl.ds(particles, extra)]))
    copies += [(cellv_ref, cellv_hbm), (force_ref, force_hbm)]
    copies = [pltpu.make_async_copy(src, dst, sem.at[i]) for i, (src, dst) in enumerate(copies)]
    for copy in copies:
        copy.start()
    for copy in copies:
        copy.wait()


def body(
    velocities, particle_cells, grid_shift, axis_index, migrate_dir, migrate_slot,
    contact_colloid, contact_particle, contact_weight, colloid_velocity,
):
    _, cx, cy, nlo = axis_index.shape
    particles = velocities.shape[1]
    units = colloid_velocity.shape[1]
    contacts = contact_weight.shape[0]
    groups = particles // 128
    cells = (cx * cy, nlo)
    if cells != (2 * HI, 128) or particles % 4096 or 6 * CAP > 16 * SLOT:
        raise ValueError("sizes")
    per = [next(p for p in sizes if groups % (8 * p) == 0) for sizes in ((8, 4), (20, 8, 4))]
    grid_mean = (3, cx, cy, nlo)
    vmem = pl.BlockSpec(memory_space=pltpu.VMEM)
    hbm = pl.BlockSpec(memory_space=pl.ANY)
    outs = (
        jax.ShapeDtypeStruct((3, groups, 128), F32),
        jax.ShapeDtypeStruct((3, 1, 6 * CAP), F32),
        jax.ShapeDtypeStruct(grid_mean, F32),
        jax.ShapeDtypeStruct((3, units), F32),
    )
    dma = pltpu.SemaphoreType.DMA

    def stay(x):
        return pltpu.with_memory_space_constraint(x, pltpu.HBM)

    kept, tail, cellv, force = pl.pallas_call(
        functools.partial(main_kernel, per, units),
        out_shape=outs,
        in_specs=[hbm] + [vmem] * 2 + [hbm] * 7,
        out_specs=(vmem,) * 4,
        scratch_shapes=[
            pltpu.VMEM((3, groups, 128), F32), pltpu.SMEM(grid_shift.shape, I32), pltpu.VMEM((3, units), F32),
            pltpu.VMEM(axis_index.shape, I32), pltpu.VMEM((groups, 128), I32), pltpu.VMEM((groups, 128), I32),
            pltpu.VMEM((1, contacts), I32), pltpu.VMEM((1, contacts), I32), pltpu.VMEM((1, contacts), F32),
            pltpu.VMEM((2,) + cells, I32), pltpu.VMEM((3,) + cells, F32), pltpu.VMEM(grid_mean, F32),
            pltpu.VMEM((2,) + cells, I32), pltpu.VMEM((8, 128), F32), pltpu.VMEM((max(per), PLANES + 1, 8, 128), F32),
            pltpu.VMEM((PLANES * HI, LO), F32), pltpu.VMEM((96, SLOT), F32), pltpu.VMEM((3, groups, 256), BF),
            pltpu.VMEM((6, 3, CAP), F32), pltpu.VMEM((6, 3, CAP), F32),
            pltpu.VMEM((6, 4, units), F32), pltpu.VMEM((6, 4, units), F32),
        ]
        + shift_scratch(axis_index.shape, I32) + shift_scratch(grid_mean, F32)
        + [dma((8,)), dma((64,)), dma((64,))],
        compiler_params=pltpu.CompilerParams(
            vmem_limit_bytes=48 * 2**20, collective_id=0, has_side_effects=True
        ),
        cost_estimate=pl.CostEstimate(flops=10**9, bytes_accessed=30_000_000, transcendentals=0),
    )(
        stay(grid_shift), velocities.reshape(3, groups, 128), particle_cells.reshape(2, groups, 128), stay(axis_index), stay(migrate_dir.reshape(groups, 128)),
        stay(migrate_slot.reshape(groups, 128)), stay(contact_particle.reshape(1, -1)),
        stay(contact_colloid.reshape(1, -1)), stay(contact_weight.reshape(1, -1)), stay(colloid_velocity),
    )
    return pl.pallas_call(
        last_kernel,
        out_shape=(
            jax.ShapeDtypeStruct(grid_mean, F32),
            jax.ShapeDtypeStruct((3, particles + 6 * CAP), F32),
            jax.ShapeDtypeStruct((3, units), F32),
        ),
        in_specs=[vmem] * 4,
        out_specs=(hbm,) * 3,
        scratch_shapes=[dma((8,))],
        compiler_params=pltpu.CompilerParams(vmem_limit_bytes=8 * 2**20),
    )(kept.reshape(3, 1, particles), tail, cellv, force)


def solution(mesh):
    flat = P(None, AXES)
    line = P(AXES)
    grid = P(None, *AXES)

    return jax.shard_map(
        body,
        mesh=mesh,
        in_specs=(flat, flat, P(), grid, line, line, line, line, line, flat),
        out_specs=(grid, flat, flat),
        check_vma=False,
    )
```
